256 devices in a mesh: lon: 16 (over y_lo, x, core), lat: 16 (over z, y_hi).
Axes of the slice: x: 4, y: 4 (y_hi: 2, y_lo: 2; y = y_hi * 2 + y_lo), z: 8, core: 2. Of those that a mesh axis runs over, the one named last changes fastest.
Arguments:
- tracers: bfloat16 [12, 64, 128, 2048], P(None, None, 'lat', 'lon'), may hold values from 0.099609375 to 2
- east_wind: bfloat16 [64, 128, 2048], P(None, 'lat', 'lon'), may hold values from -0.44921875 to 0.44921875
- north_wind: bfloat16 [64, 128, 2048], P(None, 'lat', 'lon'), may hold values from -0.44921875 to 0.44921875
- sunlit: int32 [128, 2048], P('lat', 'lon'), may hold values from 0 to 1, as said below
- coupling: float32 [12, 12], replicated, may hold values from -0.15 to 0.15
- rate_table: float32 [8, 64], replicated, may hold values from 0.01 to 0.6
- rate_index: int32 [12], replicated, may hold values from 0 to 7
- kappa: float32 [63], replicated, may hold values from 0.05 to 0.24
Outputs:
- updated: bfloat16 [12, 64, 128, 2048], P(None, None, 'lat', 'lon')
The draws below stay inside these ranges and needn't reach their ends.
Inputs may be any that keep to these rules, and one draw needn't show every extreme that they name: A device's block of columns holds at most 768 sunlit columns, and together with the block of the device half the lon axis away (same lat index) at most 1024; both bounds are reached in every draw.
All inputs are finite; a program needn't handle non-finite values.
Results may differ from the reference program's by a relative error of at most 0.001.
Values may be sent and summed in bfloat16 or wider, within the bound.
No kernel may reach another device: no remote copies, remote signals or barrier semaphores. Data moves between devices by JAX's collectives and lax.ppermute only.
A program may use at most 128 MiB of HBM per device.

```python
import math
import jax
import jax.numpy as jnp
from jax import lax

S = 12
LEV = 64
CLON = 128
CLAT = 8
SUBSTEPS = 16
RATES = 8
COLS = 1024
NLON = 2048
NLAT = 128
LON_TILES = 16
LAT_TILES = 16


def draw_sunlit(key, part):
    paired = LON_TILES // 2
    key_lead, key_rest, key_side, key_rank = jax.random.split(jax.random.fold_in(key, 11), 4)
    quarter = COLS // 4
    leading = jax.random.randint(key_lead, (LAT_TILES, paired), quarter, 3 * quarter + 1)
    leftover = COLS - leading
    trailing = jax.random.randint(key_rest, (LAT_TILES, paired), 0, leftover + 1)
    leading = leading.at[0, 0].set(3 * quarter)
    trailing = trailing.at[0, 0].set(quarter)
    sided = jax.random.randint(key_side, (LAT_TILES, paired), 0, 2)
    western = jnp.where(sided == 1, leading, trailing)
    eastern = jnp.where(sided == 1, trailing, leading)
    counted = jnp.concatenate([western, eastern], axis=1)
    scores = jax.random.randint(key_rank, (LAT_TILES, LON_TILES, COLS), 0, 2 ** 16) * COLS
    scores = scores + jnp.arange(COLS, dtype=jnp.int32)[None, None, :]
    ranking = jnp.argsort(jnp.argsort(scores, axis=-1), axis=-1)
    lit = (ranking < counted[:, :, None]).astype(jnp.int32)
    lit = lit.reshape(LAT_TILES, LON_TILES, CLAT, CLON).transpose(0, 2, 1, 3)
    return lit.reshape(NLAT, NLON)


def set_ends(entries, rng, smallest, high):
    place = [jax.random.randint(jax.random.fold_in(rng, axis), (), 0, length) for axis, length in enumerate(entries.shape)]
    widest = entries.shape.index(max(entries.shape))
    beside = place[:widest] + [(place[widest] + 1) % entries.shape[widest]] + place[widest + 1:]
    return entries.at[tuple(place)].set(smallest).at[tuple(beside)].set(high)


def block_scale(own_key, dims, pieces, smallest, top_value):
    gain = 1.0
    for axis_at, shards_of in pieces:
        draws = jax.random.uniform(jax.random.fold_in(jax.random.fold_in(own_key, 6), axis_at), (shards_of,), jnp.float32, smallest / len(pieces), top_value / len(pieces))
        gain = gain * jnp.repeat(jnp.exp(draws), dims[axis_at] // shards_of).reshape((-1,) + (1,) * (len(dims) - 1 - axis_at))
    return gain


def noise(own_key, extent, deviation, reach, held_as=jnp.bfloat16):
    entries = deviation * jax.random.normal(own_key, extent, jnp.float32)
    return jnp.clip(entries, min=-reach, max=reach).astype(held_as)


def setup_inputs(seed: int = 0) -> dict:
    arg_keys = jax.random.split(jax.random.key(seed), 9)
    tracers = jnp.clip(0.099609375 + 1.9003906 * jax.random.uniform(arg_keys[0], (S, LEV, NLAT, NLON), jnp.float32) ** block_scale(arg_keys[0], (S, LEV, NLAT, NLON), ((2, 16), (3, 16)), -0.2, 0.2), 0.099609375, 2.0).astype(jnp.bfloat16)
    east_wind = jnp.clip(jax.random.uniform(arg_keys[1], (LEV, NLAT, NLON), jnp.float32, -0.44921875, 0.44921875) * block_scale(arg_keys[1], (LEV, NLAT, NLON), ((1, 16), (2, 16)), -0.4, 0.0), -0.44921875, 0.44921875).astype(jnp.bfloat16)
    north_wind = jnp.clip(jax.random.uniform(arg_keys[2], (LEV, NLAT, NLON), jnp.float32, -0.44921875, 0.44921875) * block_scale(arg_keys[2], (LEV, NLAT, NLON), ((1, 16), (2, 16)), -0.4, 0.0), -0.44921875, 0.44921875).astype(jnp.bfloat16)
    sunlit = draw_sunlit(jax.random.fold_in(arg_keys[8], 71), 0)
    coupling = noise(arg_keys[4], (S, S), 0.03, 0.15, jnp.float32)
    rate_table = jnp.clip(jnp.exp(jax.random.uniform(arg_keys[5], (RATES, LEV), jnp.float32, math.log(0.01), math.log(0.6))), 0.01, 0.6)
    rate_index = set_ends(jax.random.randint(arg_keys[6], (S,), 0, RATES), jax.random.fold_in(arg_keys[6], 1), 0, RATES - 1).astype(jnp.int32)
    kappa = jnp.clip(jax.random.uniform(arg_keys[7], (LEV - 1,), jnp.float32, 0.05, 0.24), 0.05, 0.24)
    return {"tracers": tracers, "east_wind": east_wind, "north_wind": north_wind, "sunlit": sunlit, "coupling": coupling, "rate_table": rate_table, "rate_index": rate_index, "kappa": kappa}


def chemistry(start, coupling, loss, kappa):
    state = start.astype(jnp.float32)

    def substep(step, state):
        made = jnp.einsum('st,tlk->slk', coupling, state, precision=lax.Precision.HIGHEST)
        state = (state + made) / (1.0 + loss[:, :, None] * (1.0 + state * state))
        flux = kappa[None, :, None] * (state[:, 1:] - state[:, :-1])
        zeros = jnp.zeros_like(flux[:, :1])
        return state + jnp.concatenate([flux, zeros], axis=1) - jnp.concatenate([zeros, flux], axis=1)

    return lax.fori_loop(0, SUBSTEPS, substep, state)


def advect_species(inputs):
    conc, speed_east, speed_north = inputs
    west_cell = jnp.roll(conc, 1, axis=2)
    west_flux = jnp.maximum(speed_east, 0.0) * west_cell + jnp.minimum(speed_east, 0.0) * conc
    east_flux = jnp.roll(west_flux, -1, axis=2)
    zero_row = jnp.zeros_like(conc[:, :1])
    south_cell = jnp.concatenate([zero_row, conc[:, :-1]], axis=1)
    south_flux = jnp.maximum(speed_north, 0.0) * south_cell + jnp.minimum(speed_north, 0.0) * conc
    north_flux = jnp.concatenate([south_flux[:, 1:], zero_row], axis=1)
    return (conc - (east_flux - west_flux) - (north_flux - south_flux)).astype(jnp.bfloat16)


def reference(tracers, east_wind, north_wind, sunlit, coupling, rate_table, rate_index, kappa):
    speed_east = east_wind.astype(jnp.float32)
    speed_north = north_wind.astype(jnp.float32).at[:, 0, :].set(0.0)
    advected = lax.map(lambda conc: advect_species((conc.astype(jnp.float32), speed_east, speed_north)), tracers)
    loss = rate_table[rate_index]
    blocked = advected.reshape(S, LEV, LAT_TILES, CLAT * NLON).transpose(2, 0, 1, 3)
    light = sunlit.reshape(LAT_TILES, CLAT * NLON)

    def one_block(inputs):
        block, lit = inputs
        finished = chemistry(block, coupling, loss, kappa).astype(jnp.bfloat16)
        return jnp.where(lit[None, None, :] > 0, finished, block)

    result = lax.map(one_block, (blocked, light))
    return result.transpose(1, 2, 0, 3).reshape(S, LEV, NLAT, NLON)
```

```python
import functools

import jax
import jax.numpy as jnp
from jax import lax
from jax.experimental import pallas as pl
from jax.experimental.pallas import tpu as pltpu
from jax.sharding import PartitionSpec as P

SUBSTEPS = 16
LANES = 128
LIT_CAP = 768
CHUNK = 128
NT = (((1,), (1,)), ((), ()))


def edge_kernel(species, levels, tr, east, north, lon_out, top_out, bottom_out, rows):
    lane = lax.broadcasted_iota(jnp.int32, (8, LANES), 1)
    for s in range(species + 1):
        packed = jnp.zeros((8, LANES), jnp.float32)
        for k in range(levels):
            if s < species:
                cell = tr[s * levels + k].astype(jnp.float32)
                rows[pl.ds((s * levels + k) * 8, 8), :] = cell
            else:
                cell = east[k].astype(jnp.float32)
                rows[pl.ds((s * levels + k) * 8, 8), :] = north[k].astype(jnp.float32)
            here = (lane == 2 * k) | (lane == (2 * k - 1) % LANES)
            moved = pltpu.roll(cell, 2 * k, 1) if k else cell
            packed = jnp.where(here, moved, packed)
        lon_out[s] = packed.astype(jnp.bfloat16)
    bottom_out[...] = rows[pl.ds(0, (species + 1) * levels, stride=8), :].astype(jnp.bfloat16)
    top_out[...] = rows[pl.ds(7, species * levels, stride=8), :].astype(jnp.bfloat16)


def main_kernel(
    species,
    levels,
    groups,
    pole,
    tr,
    east,
    north,
    lit,
    from_west,
    from_east,
    from_south,
    from_north,
    mix,
    loss,
    kappa,
    out,
    lon_edge,
    south_row,
    north_row,
    adv,
    xb,
    pick,
    state,
    made,
    back,
):
    f32, bf16 = jnp.float32, jnp.bfloat16
    lane = lax.broadcasted_iota(jnp.int32, (8, LANES), 1)
    sub = lax.broadcasted_iota(jnp.int32, (8, LANES), 0)
    width = groups * LANES

    for s in range(species + 1):
        lon_edge[s] = jnp.where(
            lane % 2 == 0, from_east[s].astype(f32), pltpu.roll(from_west[s].astype(f32), 2, 1)
        )
    south_row[...] = from_south[...].astype(f32)
    north_row[...] = from_north[...].astype(f32)
    at_pole = pole[0] > 0

    slots = LANES // species
    zero_tile = jnp.zeros((8, LANES), f32)
    for r in range(groups):
        for p in range(LANES):
            k = (p // species) * groups + r
            if p >= slots * species or k >= levels:
                adv[pl.ds((r * LANES + p) * 8, 8), :] = zero_tile

    def level(k, base):
        turn = LANES - 1 - 2 * k
        u = east[k].astype(f32)
        v = north[k].astype(f32)
        v = jnp.where(jnp.logical_and(at_pole, sub == 0), 0.0, v)
        u_next = jnp.where(
            lane == LANES - 1, pltpu.roll(lon_edge[species], turn, 1), pltpu.roll(u, LANES - 1, 1)
        )
        v_next = jnp.where(
            sub == 7, north_row[pl.ds(species * levels + k, 1), :], pltpu.roll(v, 7, 0)
        )
        a_west = jnp.maximum(u, 0.0)
        a_east = -jnp.minimum(u_next, 0.0)
        a_south = jnp.maximum(v, 0.0)
        a_north = -jnp.minimum(v_next, 0.0)
        a_here = (
            1.0
            - (jnp.maximum(u_next, 0.0) - jnp.minimum(u, 0.0))
            - (jnp.maximum(v_next, 0.0) - jnp.minimum(v, 0.0))
        )
        for s in range(species):
            c = tr[s * levels + k].astype(f32)
            edge = pltpu.roll(lon_edge[s], turn, 1)
            west = jnp.where(lane == 0, edge, pltpu.roll(c, 1, 1))
            east_c = jnp.where(lane == LANES - 1, edge, pltpu.roll(c, LANES - 1, 1))
            south = jnp.where(
                sub == 0, south_row[pl.ds(s * levels + k, 1), :], pltpu.roll(c, 1, 0)
            )
            north_c = jnp.where(
                sub == 7, north_row[pl.ds(s * levels + k, 1), :], pltpu.roll(c, 7, 0)
            )
            new = (
                a_here * c
                + a_west * west
                + a_east * east_c
                + a_south * south
                + a_north * north_c
            )
            at = pl.multiple_of((base + s) * 8, 8)
            adv[pl.ds(at, 8), :] = new.astype(bf16).astype(f32)

    whole_slots = levels // groups

    def slot_body(j, carry):
        for r in range(groups):
            level(j * groups + r, r * LANES + j * species)
        return carry

    lax.fori_loop(0, whole_slots, slot_body, 0)
    for r in range(levels - whole_slots * groups):
        level(whole_slots * groups + r, r * LANES + whole_slots * species)

    lit_mask = lit[...] > 0
    lit_f = lit_mask.astype(f32)
    upper = (
        lax.broadcasted_iota(jnp.int32, (LANES, LANES), 0)
        <= lax.broadcasted_iota(jnp.int32, (LANES, LANES), 1)
    ).astype(f32)
    lower = (
        lax.broadcasted_iota(jnp.int32, (8, 8), 0) > lax.broadcasted_iota(jnp.int32, (8, 8), 1)
    ).astype(f32)
    within = jnp.dot(lit_f, upper, preferred_element_type=f32)
    before = jnp.sum(jnp.dot(lower, lit_f, preferred_element_type=f32), axis=1, keepdims=True)
    rank = jnp.where(lit_mask, within + before - 1.0, -1.0).astype(jnp.int32)

    for j in range(8):
        order = lax.broadcasted_iota(jnp.int32, (LIT_CAP, LANES), 0)
        pick[:, j * LANES : (j + 1) * LANES] = (
            (order == rank[j : j + 1, :]).astype(f32).astype(bf16)
        )
        xb[:, j * LANES : (j + 1) * LANES] = adv[pl.ds(j, width, stride=8), :].astype(bf16)

    for r in range(0, groups, 2):
        n = min(2, groups - r)
        got = lax.dot_general(
            pick[...], xb[r * LANES : (r + n) * LANES, :], NT, preferred_element_type=f32
        )
        for i in range(n):
            state[r + i] = got[:, i * LANES : (i + 1) * LANES]

    def produce(parts, i):
        stack = []
        for q in parts:
            high = q.astype(bf16)
            low = (q - high.astype(f32)).astype(bf16)
            stack.append(jnp.concatenate([high, low], axis=1))
        res = jnp.dot(jnp.concatenate(stack, axis=0), mix[...], preferred_element_type=f32)
        for r in range(groups):
            part = res[r * CHUNK : (r + 1) * CHUNK]
            made[r, i * CHUNK : (i + 1) * CHUNK, :] = part[:, :LANES] + part[:, LANES:]

    def react(i):
        at = slice(i * CHUNK, (i + 1) * CHUNK)
        y = []
        for r in range(groups):
            q = state[r, at, :]
            lo = loss[r : r + 1, :]
            y.append(made[r, at, :] / ((1.0 + lo) + lo * (q * q)))
        flux = []
        for r in range(groups):
            if r + 1 < groups:
                above = y[r + 1]
            else:
                above = pltpu.roll(y[0], LANES - species, 1)
            flux.append(kappa[r : r + 1, :] * (above - y[r]))
        res = []
        for r in range(groups):
            below = flux[r - 1] if r else pltpu.roll(flux[groups - 1], species, 1)
            q = y[r] + flux[r] - below
            state[r, at, :] = q
            res.append(q)
        return res

    chunks = LIT_CAP // CHUNK
    for i in range(chunks):
        produce([state[r, i * CHUNK : (i + 1) * CHUNK, :] for r in range(groups)], i)

    def substep(step, carry):
        for i in range(chunks):
            produce(react(i), i)
        return carry

    lax.fori_loop(0, SUBSTEPS - 1, substep, 0)
    for i in range(chunks):
        for r, q in enumerate(react(i)):
            xb[r * LANES : (r + 1) * LANES, i * CHUNK : (i + 1) * CHUNK] = q.T.astype(bf16)

    for j in range(0, 8, 2):
        got = jnp.dot(
            xb[:, :LIT_CAP], pick[:, j * LANES : (j + 2) * LANES], preferred_element_type=f32
        )
        back[pl.ds(j, width, stride=8), :] = got[:, :LANES]
        back[pl.ds(j + 1, width, stride=8), :] = got[:, LANES:]

    def finish(k, base):
        for s in range(species):
            at = pl.multiple_of((base + s) * 8, 8)
            out[s * levels + k] = jnp.where(
                lit_mask, back[pl.ds(at, 8), :], adv[pl.ds(at, 8), :]
            ).astype(bf16)

    def finish_body(j, carry):
        for r in range(groups):
            finish(j * groups + r, r * LANES + j * species)
        return carry

    lax.fori_loop(0, whole_slots, finish_body, 0)
    for r in range(levels - whole_slots * groups):
        finish(whole_slots * groups + r, r * LANES + whole_slots * species)


def spread(values, species, slots, groups):
    levels = values.shape[1]
    full = jnp.pad(values, ((0, 0), (0, slots * groups - levels)))
    full = jnp.broadcast_to(full, (species, slots * groups))
    full = full.reshape(species, slots, groups).transpose(2, 1, 0).reshape(groups, slots * species)
    return jnp.pad(full, ((0, 8 - groups), (0, LANES - slots * species)))


def local(tracers, east_wind, north_wind, sunlit, coupling, rate_table, rate_index, kappa):
    species, levels, lat_rows, lon_cols = tracers.shape
    slots = LANES // species
    groups = -(-levels // slots)
    width = groups * LANES
    f32, bf16 = jnp.float32, jnp.bfloat16
    tr = tracers.reshape(species * levels, lat_rows, lon_cols)
    vmem = pl.BlockSpec(memory_space=pltpu.VMEM)
    lon_pack, top, bottom = pl.pallas_call(
        functools.partial(edge_kernel, species, levels),
        out_shape=(
            jax.ShapeDtypeStruct((species + 1, 8, LANES), bf16),
            jax.ShapeDtypeStruct((species * levels, LANES), bf16),
            jax.ShapeDtypeStruct(((species + 1) * levels, LANES), bf16),
        ),
        in_specs=[vmem] * 3,
        out_specs=(vmem,) * 3,
        scratch_shapes=[pltpu.VMEM(((species + 1) * levels * 8, LANES), f32)],
        name="edges",
    )(tr, east_wind, north_wind)

    nlon, nlat = lax.axis_size("lon"), lax.axis_size("lat")
    from_west = lax.ppermute(lon_pack, "lon", [(i, (i + 1) % nlon) for i in range(nlon)])
    from_east = lax.ppermute(lon_pack, "lon", [((i + 1) % nlon, i) for i in range(nlon)])
    from_south = lax.ppermute(top, "lat", [(i, i + 1) for i in range(nlat - 1)])
    from_north = lax.ppermute(bottom, "lat", [(i + 1, i) for i in range(nlat - 1)])

    rows = rate_table.shape[0]
    picker = (rate_index[:, None] == jnp.arange(rows, dtype=jnp.int32)[None, :]).astype(f32)
    loss = jnp.sum(picker[:, :, None] * rate_table[None, :, :], axis=1)
    loss = spread(loss, species, slots, groups)
    kap = spread(jnp.pad(kappa, (0, 1))[None], species, slots, groups)
    full = coupling.T + jnp.eye(species, dtype=f32)
    high = lax.reduce_precision(full, 8, 7)
    low = full - high
    row = jnp.arange(LANES)
    same = (row[:, None] // species == row[None, :] // species) & (row < slots * species)[None, :]

    def block(part):
        wide = jnp.pad(jnp.tile(part, (slots, slots)), ((0, LANES - slots * species),) * 2)
        return jnp.where(same, wide, 0.0)

    half = jnp.concatenate([block(high), block(low)], axis=1).astype(bf16)
    mix = jnp.concatenate([half, half], axis=0)
    pole = (lax.axis_index("lat") == 0).astype(jnp.int32).reshape(1)

    out = pl.pallas_call(
        functools.partial(main_kernel, species, levels, groups),
        out_shape=jax.ShapeDtypeStruct((species * levels, lat_rows, lon_cols), bf16),
        in_specs=[pl.BlockSpec(memory_space=pltpu.SMEM)] + [vmem] * 11,
        out_specs=vmem,
        scratch_shapes=[
            pltpu.VMEM((species + 1, 8, LANES), f32),
            pltpu.VMEM((species * levels, LANES), f32),
            pltpu.VMEM(((species + 1) * levels, LANES), f32),
            pltpu.VMEM((width * 8, LANES), f32),
            pltpu.VMEM((width, 8 * LANES), bf16),
            pltpu.VMEM((LIT_CAP, 8 * LANES), bf16),
            pltpu.VMEM((groups, LIT_CAP, LANES), f32),
            pltpu.VMEM((groups, LIT_CAP, LANES), f32),
            pltpu.VMEM((width * 8, LANES), f32),
        ],
        name="step",
    )(
        pole,
        tr,
        east_wind,
        north_wind,
        sunlit,
        from_west,
        from_east,
        from_south,
        from_north,
        mix,
        loss,
        kap,
    )
    return out.reshape(tracers.shape)


def solution(mesh):
    placed = (
        P(None, None, "lat", "lon"),
        P(None, "lat", "lon"),
        P(None, "lat", "lon"),
        P("lat", "lon"),
        P(),
        P(),
        P(),
        P(),
    )
    return jax.shard_map(
        local, mesh=mesh, in_specs=placed, out_specs=P(None, None, "lat", "lon"), check_vma=False
    )
```

```python
import functools

import jax
import jax.numpy as jnp
from jax import lax
from jax.experimental import pallas as pl
from jax.experimental.pallas import tpu as pltpu
from jax.sharding import PartitionSpec as P

SUBSTEPS = 16
LANES = 128
LIT_CAP = 768
FIRST = 512
CHUNK = 64
VMEM_LIMIT = 24 << 20
NT = (((1,), (1,)), ((), ()))
f32, bf16 = jnp.float32, jnp.bfloat16


def iota(shape, axis):
    return lax.broadcasted_iota(jnp.int32, shape, axis)


def place(k, s, species, groups):
    return (k % groups) * LANES + (k // groups) * species + s


def edge_kernel(species, levels, groups, tr, east, north, lon_out, top_out, bottom_out, rows, vrow):
    lane = iota((8, LANES), 1)
    zero = jnp.zeros((8, LANES), f32)
    for r in range(groups):
        for p in range(LANES):
            if p >= (LANES // species) * species or (p // species) * groups + r >= levels:
                rows[pl.ds((r * LANES + p) * 8, 8), :] = zero
    for s in range(species + 1):
        packed = zero
        for k in range(levels):
            if s < species:
                cell = tr[s * levels + k].astype(f32)
                rows[pl.ds(place(k, s, species, groups) * 8, 8), :] = cell
            else:
                cell = east[k].astype(f32)
                vrow[pl.ds(k * 8, 8), :] = north[k].astype(f32)
            here = (lane == 2 * k) | (lane == (2 * k - 1) % LANES)
            moved = pltpu.roll(cell, 2 * k, 1) if k else cell
            packed = jnp.where(here, moved, packed)
        lon_out[s] = packed.astype(bf16)
    width = groups * LANES
    bottom_out[:width] = rows[pl.ds(0, width, stride=8), :].astype(bf16)
    bottom_out[width:] = vrow[pl.ds(0, levels, stride=8), :].astype(bf16)
    top_out[...] = rows[pl.ds(7, width, stride=8), :].astype(bf16)


def run_chemistry(groups, species, count, mix, loss, kappa, state, made, emit):
    def produce(parts, i):
        stack = []
        for q in parts:
            high = q.astype(bf16)
            low = (q - high.astype(f32)).astype(bf16)
            stack.append(jnp.concatenate([high, low], axis=1))
        res = jnp.dot(jnp.concatenate(stack, axis=0), mix[...], preferred_element_type=f32)
        for r in range(groups):
            part = res[r * CHUNK : (r + 1) * CHUNK]
            made[r, i * CHUNK : (i + 1) * CHUNK, :] = part[:, :LANES] + part[:, LANES:]

    def react(i):
        at = slice(i * CHUNK, (i + 1) * CHUNK)
        y = []
        for r in range(groups):
            q = state[r, at, :]
            lo = loss[r : r + 1, :]
            y.append(made[r, at, :] / ((1.0 + lo) + lo * (q * q)))
        flux = []
        for r in range(groups):
            if r + 1 < groups:
                above = y[r + 1]
            else:
                above = pltpu.roll(y[0], LANES - species, 1)
            flux.append(kappa[r : r + 1, :] * (above - y[r]))
        res = []
        for r in range(groups):
            below = flux[r - 1] if r else pltpu.roll(flux[groups - 1], species, 1)
            q = y[r] + flux[r] - below
            state[r, at, :] = q
            res.append(q)
        return res

    chunks = count // CHUNK
    for i in range(chunks):
        produce([state[r, i * CHUNK : (i + 1) * CHUNK, :] for r in range(groups)], i)

    def substep(step, carry):
        for i in range(chunks):
            produce(react(i), i)
        return carry

    lax.fori_loop(0, SUBSTEPS - 1, substep, 0)
    for i in range(chunks):
        react(i)
    for r in range(groups):
        emit(r, state[r, :count, :].T.astype(bf16))


def tables(species, levels, groups, coupling, rate_table, rate_index, kappa, mix, tab, loss_rows):
    slots = LANES // species
    for s in range(species):
        loss_rows[s : s + 1, :] = rate_table[pl.ds(rate_index[s], 1), :]
    p = iota((LANES, species), 0)
    slot = (p * 171) >> 11
    spread = jnp.logical_and(p - slot * species == iota((LANES, species), 1), slot < slots)
    spread = spread.astype(f32)
    full = coupling[...] + (iota((species, species), 0) == iota((species, species), 1)).astype(f32)
    same = ((iota((LANES, LANES), 0) * 171) >> 11) == ((iota((LANES, LANES), 1) * 171) >> 11)

    def block(part):
        half = lax.dot_general(spread, part.astype(f32), NT, preferred_element_type=f32)
        wide = lax.dot_general(half, spread, NT, preferred_element_type=f32)
        return jnp.where(same, wide, 0.0).astype(bf16)

    high = full.astype(bf16)
    low = (full - high.astype(f32)).astype(bf16)
    for at in (0, LANES):
        mix[at : at + LANES, :LANES] = block(high)
        mix[at : at + LANES, LANES:] = block(low)
    width = groups * LANES
    col = iota((levels, width), 1)
    lane = col & (LANES - 1)
    slot = (lane * 171) >> 11
    sel = jnp.logical_and(iota((levels, width), 0) == slot * groups + (col >> 7), slot < slots)
    sel = sel.astype(f32)
    exact = lax.Precision.HIGHEST
    spread_loss = jnp.dot(loss_rows[...], sel, preferred_element_type=f32, precision=exact)
    col = iota((species, width), 1) & (LANES - 1)
    mine = col - ((col * 171) >> 11) * species == iota((species, width), 0)
    loss = jnp.sum(jnp.where(mine, spread_loss, 0.0), axis=0, keepdims=True)
    kap = jnp.dot(kappa[...], sel, preferred_element_type=f32, precision=exact)
    for r in range(groups):
        tab[r : r + 1, :] = loss[:, r * LANES : (r + 1) * LANES]
        tab[8 + r : 9 + r, :] = kap[:, r * LANES : (r + 1) * LANES]


def first_kernel(
    species,
    levels,
    groups,
    pole,
    rate_index,
    tr,
    east,
    north,
    lit,
    from_west,
    from_east,
    coupling,
    rate_table,
    kappa,
    part_out,
    xb,
    pick,
    fin,
    mix,
    tab,
    lon_edge,
    adv,
    state,
    made,
    loss_rows,
):
    lane = iota((8, LANES), 1)
    sub = iota((8, LANES), 0)
    width = groups * LANES
    slots = LANES // species

    tables(species, levels, groups, coupling, rate_table, rate_index, kappa, mix, tab, loss_rows)
    for s in range(species + 1):
        lon_edge[s] = jnp.where(
            lane % 2 == 0, from_east[s].astype(f32), pltpu.roll(from_west[s].astype(f32), 2, 1)
        )
    at_pole = pole[0] > 0

    zero_tile = jnp.zeros((8, LANES), f32)
    for r in range(groups):
        for p in range(LANES):
            if p >= slots * species or (p // species) * groups + r >= levels:
                adv[pl.ds((r * LANES + p) * 8, 8), :] = zero_tile

    def level(k, base):
        turn = LANES - 1 - 2 * k
        u = east[k].astype(f32)
        v = north[k].astype(f32)
        v = jnp.where(jnp.logical_and(at_pole, sub == 0), 0.0, v)
        u_next = jnp.where(
            lane == LANES - 1, pltpu.roll(lon_edge[species], turn, 1), pltpu.roll(u, LANES - 1, 1)
        )
        v_next = jnp.where(sub == 7, 0.0, pltpu.roll(v, 7, 0))
        a_west = jnp.maximum(u, 0.0)
        a_east = -jnp.minimum(u_next, 0.0)
        a_south = jnp.where(sub == 0, 0.0, jnp.maximum(v, 0.0))
        a_north = -jnp.minimum(v_next, 0.0)
        a_here = (
            1.0
            - (jnp.maximum(u_next, 0.0) - jnp.minimum(u, 0.0))
            - (jnp.maximum(v_next, 0.0) - jnp.minimum(v, 0.0))
        )
        for s in range(species):
            c = tr[s * levels + k].astype(f32)
            edge = pltpu.roll(lon_edge[s], turn, 1)
            west = jnp.where(lane == 0, edge, pltpu.roll(c, 1, 1))
            east_c = jnp.where(lane == LANES - 1, edge, pltpu.roll(c, LANES - 1, 1))
            new = (
                a_here * c
                + a_west * west
                + a_east * east_c
                + a_south * pltpu.roll(c, 1, 0)
                + a_north * pltpu.roll(c, 7, 0)
            )
            at = pl.multiple_of((base + s) * 8, 8)
            adv[pl.ds(at, 8), :] = new

    whole_slots = levels // groups

    def slot_body(j, carry):
        for r in range(groups):
            level(j * groups + r, r * LANES + j * species)
        return carry

    lax.fori_loop(0, whole_slots, slot_body, 0)
    for r in range(levels - whole_slots * groups):
        level(whole_slots * groups + r, r * LANES + whole_slots * species)

    lit_mask = lit[...] > 0
    inner = jnp.logical_and(sub > 0, sub < 7)
    upper = (iota((LANES, LANES), 0) <= iota((LANES, LANES), 1)).astype(f32)
    lower = (iota((8, 8), 0) > iota((8, 8), 1)).astype(f32)

    def rank_of(mask):
        ones = mask.astype(f32)
        within = jnp.dot(ones, upper, preferred_element_type=f32)
        before = jnp.sum(jnp.dot(lower, ones, preferred_element_type=f32), axis=1, keepdims=True)
        return within + before - 1.0

    inner_rank = rank_of(jnp.logical_and(lit_mask, inner))
    outer_lit = jnp.logical_and(lit_mask, jnp.logical_not(inner))
    outer_rank = rank_of(outer_lit)
    outer_count = jnp.sum(outer_lit.astype(f32))
    slot = jnp.where(
        inner,
        inner_rank + jnp.where(inner_rank >= FIRST, outer_count, 0.0),
        outer_rank + FIRST,
    )
    slot = jnp.where(lit_mask, slot, -1.0).astype(jnp.int32)

    order = iota((LIT_CAP, LANES), 0)
    for j in range(8):
        pick[:, j * LANES : (j + 1) * LANES] = (
            (order == slot[j : j + 1, :]).astype(f32).astype(bf16)
        )
        rows = adv[pl.ds(j, width, stride=8), :]
        if 0 < j < 7:
            xb[:, j * LANES : (j + 1) * LANES] = rows.astype(bf16)
        else:
            xb[:, j * LANES : (j + 1) * LANES] = jnp.zeros((width, LANES), bf16)
            part_out[j // 7] = rows

    span = slice(LANES, 7 * LANES)
    for r in range(0, groups, 2):
        n = min(2, groups - r)
        got = lax.dot_general(
            pick[:FIRST, span],
            xb[r * LANES : (r + n) * LANES, span],
            NT,
            preferred_element_type=f32,
        )
        for i in range(n):
            state[r + i] = got[:, i * LANES : (i + 1) * LANES]

    def emit(r, value):
        fin[r * LANES : (r + 1) * LANES, :] = value

    run_chemistry(groups, species, FIRST, mix, tab, tab.at[8:16], state, made, emit)


def second_kernel(
    species,
    levels,
    groups,
    pole,
    part,
    top,
    bottom,
    from_south,
    from_north,
    xb,
    pick,
    fin,
    mix,
    tab,
    lit,
    out,
    xe,
    fin_b,
    state,
    made,
    back,
):
    width = groups * LANES
    slots = LANES // species
    lit_mask = lit[...] > 0
    row = iota((width, levels), 0)
    slot = ((row & (LANES - 1)) * 171) >> 11
    sel = jnp.logical_and(iota((width, levels), 1) == slot * groups + (row >> 7), slot < slots)
    sel = sel.astype(f32).astype(bf16)
    v_here = jnp.dot(sel, bottom[width:, :], preferred_element_type=f32)
    v_here = jnp.where(pole[0] > 0, 0.0, jnp.maximum(v_here, 0.0))
    xe[:, :LANES] = (part[0] + v_here * from_south[...].astype(f32)).astype(bf16)
    v_next = jnp.dot(sel, from_north[width:, :], preferred_element_type=f32)
    xe[:, LANES:] = (
        part[1]
        - jnp.maximum(v_next, 0.0) * top[...].astype(f32)
        - jnp.minimum(v_next, 0.0) * from_north[:width, :].astype(f32)
    ).astype(bf16)

    rest = slice(FIRST, LIT_CAP)
    span = slice(LANES, 7 * LANES)
    for r in range(0, groups, 2):
        n = min(2, groups - r)
        rows = slice(r * LANES, (r + n) * LANES)
        got = lax.dot_general(pick[rest, span], xb[rows, span], NT, preferred_element_type=f32)
        got = got + lax.dot_general(
            pick[rest, :LANES], xe[rows, :LANES], NT, preferred_element_type=f32
        )
        got = got + lax.dot_general(
            pick[rest, 7 * LANES :], xe[rows, LANES:], NT, preferred_element_type=f32
        )
        for i in range(n):
            state[r + i] = got[:, i * LANES : (i + 1) * LANES]

    def emit(r, value):
        fin_b[r * LANES : (r + 1) * LANES, :] = value

    run_chemistry(groups, species, LIT_CAP - FIRST, mix, tab, tab.at[8:16], state, made, emit)

    def settle(j, got, moved):
        keep = lit_mask[j : j + 1, :]
        back[pl.ds(j, width, stride=8), :] = jnp.where(keep, got, moved.astype(f32))

    for j in range(1, 7, 2):
        cols = slice(j * LANES, (j + 2) * LANES)
        got = jnp.dot(fin[...], pick[:FIRST, cols], preferred_element_type=f32)
        got = got + jnp.dot(fin_b[...], pick[rest, cols], preferred_element_type=f32)
        settle(j, got[:, :LANES], xb[:, j * LANES : (j + 1) * LANES])
        settle(j + 1, got[:, LANES:], xb[:, (j + 1) * LANES : (j + 2) * LANES])
    for i, j in enumerate((0, 7)):
        got = jnp.dot(
            fin_b[...], pick[rest, j * LANES : (j + 1) * LANES], preferred_element_type=f32
        )
        settle(j, got, xe[:, i * LANES : (i + 1) * LANES])

    def finish(k, base):
        for s in range(species):
            at = pl.multiple_of((base + s) * 8, 8)
            out[s * levels + k] = back[pl.ds(at, 8), :].astype(bf16)

    whole_slots = levels // groups

    def finish_body(j, carry):
        for r in range(groups):
            finish(j * groups + r, r * LANES + j * species)
        return carry

    lax.fori_loop(0, whole_slots, finish_body, 0)
    for r in range(levels - whole_slots * groups):
        finish(whole_slots * groups + r, r * LANES + whole_slots * species)


def local(tracers, east_wind, north_wind, sunlit, coupling, rate_table, rate_index, kappa):
    species, levels, lat_rows, lon_cols = tracers.shape
    slots = LANES // species
    groups = -(-levels // slots)
    width = groups * LANES
    sizes = (species, levels, groups)
    tr = tracers.reshape(species * levels, lat_rows, lon_cols)
    vmem = pl.BlockSpec(memory_space=pltpu.VMEM)
    smem = pl.BlockSpec(memory_space=pltpu.SMEM)
    shape = jax.ShapeDtypeStruct
    lon_pack, top, bottom = pl.pallas_call(
        functools.partial(edge_kernel, *sizes),
        out_shape=(
            shape((species + 1, 8, LANES), bf16),
            shape((width, LANES), bf16),
            shape((width + levels, LANES), bf16),
        ),
        in_specs=[vmem] * 3,
        out_specs=(vmem,) * 3,
        scratch_shapes=[pltpu.VMEM((width * 8, LANES), f32), pltpu.VMEM((levels * 8, LANES), f32)],
        name="edges",
    )(tr, east_wind, north_wind)

    nlon, nlat = lax.axis_size("lon"), lax.axis_size("lat")
    from_south = lax.ppermute(top, "lat", [(i, i + 1) for i in range(nlat - 1)])
    from_north = lax.ppermute(bottom, "lat", [(i + 1, i) for i in range(nlat - 1)])
    from_west = lax.ppermute(lon_pack, "lon", [(i, (i + 1) % nlon) for i in range(nlon)])
    from_east = lax.ppermute(lon_pack, "lon", [((i + 1) % nlon, i) for i in range(nlon)])
    pole = (lax.axis_index("lat") == 0).astype(jnp.int32).reshape(1)

    part, xb, pick, fin, mix, tab = pl.pallas_call(
        functools.partial(first_kernel, *sizes),
        out_shape=(
            shape((2, width, LANES), f32),
            shape((width, 8 * LANES), bf16),
            shape((LIT_CAP, 8 * LANES), bf16),
            shape((width, FIRST), bf16),
            shape((2 * LANES, 2 * LANES), bf16),
            shape((16, LANES), f32),
        ),
        in_specs=[smem] * 2 + [vmem] * 9,
        out_specs=(vmem,) * 6,
        scratch_shapes=[
            pltpu.VMEM((species + 1, 8, LANES), f32),
            pltpu.VMEM((width * 8, LANES), f32),
            pltpu.VMEM((groups, FIRST, LANES), f32),
            pltpu.VMEM((groups, FIRST, LANES), f32),
            pltpu.VMEM((species, levels), f32),
        ],
        cost_estimate=pl.CostEstimate(
            flops=20_000_000_000, bytes_accessed=8_000_000, transcendentals=0
        ),
        compiler_params=pltpu.CompilerParams(vmem_limit_bytes=VMEM_LIMIT),
        name="first",
    )(
        pole,
        rate_index,
        tr,
        east_wind,
        north_wind,
        sunlit,
        from_west,
        from_east,
        coupling,
        rate_table,
        jnp.pad(kappa, (0, 1)).reshape(1, levels),
    )

    count = LIT_CAP - FIRST
    out = pl.pallas_call(
        functools.partial(second_kernel, *sizes),
        out_shape=shape((species * levels, lat_rows, lon_cols), bf16),
        in_specs=[smem] + [vmem] * 11,
        out_specs=vmem,
        scratch_shapes=[
            pltpu.VMEM((width, 2 * LANES), bf16),
            pltpu.VMEM((width, count), bf16),
            pltpu.VMEM((groups, count, LANES), f32),
            pltpu.VMEM((groups, count, LANES), f32),
            pltpu.VMEM((width * 8, LANES), f32),
        ],
        compiler_params=pltpu.CompilerParams(vmem_limit_bytes=VMEM_LIMIT),
        name="second",
    )(pole, part, top, bottom, from_south, from_north, xb, pick, fin, mix, tab, sunlit)
    return out.reshape(tracers.shape)


def solution(mesh):
    placed = (
        P(None, None, "lat", "lon"),
        P(None, "lat", "lon"),
        P(None, "lat", "lon"),
        P("lat", "lon"),
        P(),
        P(),
        P(),
        P(),
    )
    return jax.shard_map(
        local, mesh=mesh, in_specs=placed, out_specs=P(None, None, "lat", "lon"), check_vma=False
    )
```

```python
import functools

import jax
import jax.numpy as jnp
from jax import lax
from jax.experimental import pallas as pl
from jax.experimental.pallas import tpu as pltpu
from jax.sharding import PartitionSpec as P

SUBSTEPS = 16
LANES = 128
LIT_CAP = 768
FIRST = 512
CHUNK_FIRST = 256
CHUNK_SECOND = 128
UNROLL = 3
VMEM_LIMIT = 24 << 20
NT = (((1,), (1,)), ((), ()))
f32, bf16 = jnp.float32, jnp.bfloat16


def iota(shape, axis):
    return lax.broadcasted_iota(jnp.int32, shape, axis)


def place(k, s, species, groups):
    return (k % groups) * LANES + (k // groups) * species + s


def edge_kernel(
    species,
    levels,
    groups,
    tr,
    east,
    north,
    lon_out,
    lat_a,
    lat_b,
    top_out,
    wind_out,
    rows,
    vrow,
):
    lane = iota((8, LANES), 1)
    zero = jnp.zeros((8, LANES), f32)
    for r in range(groups):
        for p in range(LANES):
            if p >= (LANES // species) * species or (p // species) * groups + r >= levels:
                rows[pl.ds((r * LANES + p) * 8, 8), :] = zero
    for k in range(levels):
        vrow[pl.ds(k * 8, 8), :] = north[k].astype(f32)
    for s in range(species + 1):
        packed = zero
        for k in range(levels):
            if s < species:
                cell = tr[s * levels + k].astype(f32)
                rows[pl.ds(place(k, s, species, groups) * 8, 8), :] = cell
            else:
                cell = east[k].astype(f32)
            here = (lane == 2 * k) | (lane == (2 * k - 1) % LANES)
            moved = pltpu.roll(cell, 2 * k, 1) if k else cell
            packed = jnp.where(here, moved, packed)
        lon_out[s] = packed.astype(bf16)
    width = groups * LANES
    is_odd = lax.axis_index("lat") % 2 > 0
    bottom = rows[pl.ds(0, width, stride=8), :]
    top = rows[pl.ds(7, width, stride=8), :]
    wind = vrow[pl.ds(0, levels, stride=8), :].astype(bf16)
    lat_a[:width] = jnp.where(is_odd, bottom, top).astype(bf16)
    lat_b[:width] = jnp.where(is_odd, top, bottom).astype(bf16)
    lat_a[width:] = wind
    lat_b[width:] = wind
    wind_out[...] = wind
    top_out[...] = top.astype(bf16)


def run_chemistry(groups, species, count, size, mix, tab, state, made, emit):
    kappa = tab.at[8:16]

    def produce(parts, i):
        for r, q in enumerate(parts):
            high = q.astype(bf16)
            low = (q - high.astype(f32)).astype(bf16)
            pair = jnp.concatenate([high, low], axis=1)
            res = jnp.dot(pair, mix[r], preferred_element_type=f32)
            made[r, i * size : (i + 1) * size, :] = res[:, :LANES] + res[:, LANES:]

    def react(i):
        at = slice(i * size, (i + 1) * size)
        y = []
        for r in range(groups):
            q = state[r, at, :]
            y.append(made[r, at, :] / (tab[r : r + 1, :] + q * q))
        flux = []
        for r in range(groups):
            if r + 1 < groups:
                above = y[r + 1]
            else:
                above = pltpu.roll(y[0], LANES - species, 1)
            flux.append(kappa[r : r + 1, :] * (above - y[r]))
        res = []
        for r in range(groups):
            below = flux[r - 1] if r else pltpu.roll(flux[groups - 1], species, 1)
            q = y[r] + flux[r] - below
            state[r, at, :] = q
            res.append(q)
        return res

    chunks = count // size
    for i in range(chunks):
        produce([state[r, i * size : (i + 1) * size, :] for r in range(groups)], i)

    def substep(step, carry):
        for _ in range(UNROLL):
            for i in range(chunks):
                produce(react(i), i)
        return carry

    lax.fori_loop(0, (SUBSTEPS - 1) // UNROLL, substep, 0)
    for i in range(chunks):
        react(i)
    for r in range(groups):
        emit(r, state[r, :count, :].T.astype(bf16))


def tables(species, levels, groups, small, rate_index, mix, tab, loss_rows):
    slots, rates = LANES // species, small.shape[0] - 1
    for s in range(species):
        loss_rows[s : s + 1, :] = small[pl.ds(species + rate_index[s], 1), :]
    p = iota((LANES, species), 0)
    slot = (p * 171) >> 11
    spread = jnp.logical_and(p - slot * species == iota((LANES, species), 1), slot < slots)
    spread = spread.astype(f32)
    full = small[:species, :species] + (iota((species, species), 0) == iota((species, species), 1)).astype(f32)
    same = ((iota((LANES, LANES), 0) * 171) >> 11) == ((iota((LANES, LANES), 1) * 171) >> 11)

    def block(part):
        half = lax.dot_general(spread, part.astype(f32), NT, preferred_element_type=f32)
        wide = lax.dot_general(half, spread, NT, preferred_element_type=f32)
        return jnp.where(same, wide, 0.0)

    high = full.astype(bf16)
    whole = block(high) + block((full - high.astype(f32)).astype(bf16))
    width = groups * LANES
    col = iota((levels, width), 1)
    lane = col & (LANES - 1)
    slot = (lane * 171) >> 11
    sel = jnp.logical_and(iota((levels, width), 0) == slot * groups + (col >> 7), slot < slots)
    sel = sel.astype(f32)
    exact = lax.Precision.HIGHEST
    spread_loss = jnp.dot(loss_rows[...], sel, preferred_element_type=f32, precision=exact)
    col = iota((species, width), 1) & (LANES - 1)
    mine = col - ((col * 171) >> 11) * species == iota((species, width), 0)
    loss = jnp.sum(jnp.where(mine, spread_loss, 0.0), axis=0, keepdims=True)
    kap = jnp.dot(small[rates:, :], sel, preferred_element_type=f32, precision=exact)
    inverse = jnp.where(loss > 0.0, 1.0 / jnp.where(loss > 0.0, loss, 1.0), 0.0)
    for r in range(groups):
        mine = inverse[:, r * LANES : (r + 1) * LANES]
        tab[r : r + 1, :] = 1.0 + mine
        tab[8 + r : 9 + r, :] = kap[:, r * LANES : (r + 1) * LANES]
        scaled = whole * mine
        high = scaled.astype(bf16)
        low = (scaled - high.astype(f32)).astype(bf16)
        for at in (0, LANES):
            mix[r, at : at + LANES, :LANES] = high
            mix[r, at : at + LANES, LANES:] = low


def first_kernel(
    species,
    levels,
    groups,
    rate_index,
    tr,
    east,
    north,
    lit,
    lon_a,
    lon_b,
    small,
    part_out,
    xb,
    pick,
    fin,
    mix,
    tab,
    lon_edge,
    adv,
    state,
    made,
    loss_rows,
):
    lane = iota((8, LANES), 1)
    sub = iota((8, LANES), 0)
    width = groups * LANES
    slots = LANES // species

    tables(species, levels, groups, small, rate_index, mix, tab, loss_rows)
    is_odd = lax.axis_index("lon") % 2 > 0
    for s in range(species + 1):
        got_a, got_b = lon_a[s].astype(f32), lon_b[s].astype(f32)
        from_east = jnp.where(is_odd, got_b, got_a)
        from_west = jnp.where(is_odd, got_a, got_b)
        lon_edge[s] = jnp.where(lane % 2 == 0, from_east, pltpu.roll(from_west, 2, 1))
    at_pole = lax.axis_index("lat") == 0

    zero_tile = jnp.zeros((8, LANES), f32)
    for r in range(groups):
        for p in range(LANES):
            if p >= slots * species or (p // species) * groups + r >= levels:
                adv[pl.ds((r * LANES + p) * 8, 8), :] = zero_tile

    def level(k, base):
        turn = LANES - 1 - 2 * k
        u = east[k].astype(f32)
        v = north[k].astype(f32)
        v = jnp.where(jnp.logical_and(at_pole, sub == 0), 0.0, v)
        u_next = jnp.where(
            lane == LANES - 1, pltpu.roll(lon_edge[species], turn, 1), pltpu.roll(u, LANES - 1, 1)
        )
        v_next = jnp.where(sub == 7, 0.0, pltpu.roll(v, 7, 0))
        a_west = jnp.maximum(u, 0.0)
        a_east = -jnp.minimum(u_next, 0.0)
        a_south = jnp.where(sub == 0, 0.0, jnp.maximum(v, 0.0))
        a_north = -jnp.minimum(v_next, 0.0)
        a_here = (
            1.0
            - (jnp.maximum(u_next, 0.0) - jnp.minimum(u, 0.0))
            - (jnp.maximum(v_next, 0.0) - jnp.minimum(v, 0.0))
        )
        for s in range(species):
            c = tr[s * levels + k].astype(f32)
            edge = pltpu.roll(lon_edge[s], turn, 1)
            west = jnp.where(lane == 0, edge, pltpu.roll(c, 1, 1))
            east_c = jnp.where(lane == LANES - 1, edge, pltpu.roll(c, LANES - 1, 1))
            new = (
                a_here * c
                + a_west * west
                + a_east * east_c
                + a_south * pltpu.roll(c, 1, 0)
                + a_north * pltpu.roll(c, 7, 0)
            )
            at = pl.multiple_of((base + s) * 8, 8)
            adv[pl.ds(at, 8), :] = new

    whole_slots = levels // groups

    def slot_body(j, carry):
        for r in range(groups):
            level(j * groups + r, r * LANES + j * species)
        return carry

    lax.fori_loop(0, whole_slots, slot_body, 0)
    for r in range(levels - whole_slots * groups):
        level(whole_slots * groups + r, r * LANES + whole_slots * species)

    lit_mask = lit[...] > 0
    inner = jnp.logical_and(sub > 0, sub < 7)
    upper = (iota((LANES, LANES), 0) <= iota((LANES, LANES), 1)).astype(f32)
    lower = (iota((8, 8), 0) > iota((8, 8), 1)).astype(f32)

    def rank_of(mask):
        ones = mask.astype(f32)
        within = jnp.dot(ones, upper, preferred_element_type=f32)
        before = jnp.sum(jnp.dot(lower, ones, preferred_element_type=f32), axis=1, keepdims=True)
        return within + before - 1.0

    inner_rank = rank_of(jnp.logical_and(lit_mask, inner))
    outer_lit = jnp.logical_and(lit_mask, jnp.logical_not(inner))
    outer_rank = rank_of(outer_lit)
    outer_count = jnp.sum(outer_lit.astype(f32))
    slot = jnp.where(
        inner,
        inner_rank + jnp.where(inner_rank >= FIRST, outer_count, 0.0),
        outer_rank + FIRST,
    )
    slot = jnp.where(lit_mask, slot, -1.0).astype(jnp.int32)

    order = iota((LIT_CAP, LANES), 0)
    for j in range(8):
        pick[:, j * LANES : (j + 1) * LANES] = (
            (order == slot[j : j + 1, :]).astype(f32).astype(bf16)
        )
        rows = adv[pl.ds(j, width, stride=8), :]
        if 0 < j < 7:
            xb[:, j * LANES : (j + 1) * LANES] = rows.astype(bf16)
        else:
            xb[:, j * LANES : (j + 1) * LANES] = jnp.zeros((width, LANES), bf16)
            part_out[j // 7] = rows

    span = slice(LANES, 7 * LANES)
    for r in range(0, groups, 2):
        n = min(2, groups - r)
        got = lax.dot_general(
            pick[:FIRST, span],
            xb[r * LANES : (r + n) * LANES, span],
            NT,
            preferred_element_type=f32,
        )
        for i in range(n):
            state[r + i] = got[:, i * LANES : (i + 1) * LANES]

    def emit(r, value):
        fin[r * LANES : (r + 1) * LANES, :] = value

    run_chemistry(groups, species, FIRST, CHUNK_FIRST, mix, tab, state, made, emit)


def second_kernel(
    species,
    levels,
    groups,
    part,
    top,
    wind,
    lat_a,
    lat_b,
    xb,
    pick,
    fin,
    mix,
    tab,
    lit,
    out,
    xe,
    fin_b,
    state,
    made,
    back,
):
    width = groups * LANES
    slots = LANES // species
    lit_mask = lit[...] > 0
    row = iota((width, levels), 0)
    slot = ((row & (LANES - 1)) * 171) >> 11
    sel = jnp.logical_and(iota((width, levels), 1) == slot * groups + (row >> 7), slot < slots)
    sel = sel.astype(f32).astype(bf16)
    is_odd = lax.axis_index("lat") % 2 > 0
    got_a, got_b = lat_a[:width].astype(f32), lat_b[:width].astype(f32)
    south = jnp.where(is_odd, got_a, got_b)
    north = jnp.where(is_odd, got_b, got_a)
    v_here = jnp.dot(sel, wind[...], preferred_element_type=f32)
    v_here = jnp.where(lax.axis_index("lat") == 0, 0.0, jnp.maximum(v_here, 0.0))
    xe[:, :LANES] = (part[0] + v_here * south).astype(bf16)
    wind_a, wind_b = lat_a[width:].astype(f32), lat_b[width:].astype(f32)
    v_next = jnp.where(is_odd, wind_b, wind_a).astype(bf16)
    v_next = jnp.dot(sel, v_next, preferred_element_type=f32)
    xe[:, LANES:] = (
        part[1] - jnp.maximum(v_next, 0.0) * top[...].astype(f32) - jnp.minimum(v_next, 0.0) * north
    ).astype(bf16)

    rest = slice(FIRST, LIT_CAP)
    span = slice(LANES, 7 * LANES)
    for r in range(0, groups, 2):
        n = min(2, groups - r)
        rows = slice(r * LANES, (r + n) * LANES)
        got = lax.dot_general(pick[rest, span], xb[rows, span], NT, preferred_element_type=f32)
        got = got + lax.dot_general(
            pick[rest, :LANES], xe[rows, :LANES], NT, preferred_element_type=f32
        )
        got = got + lax.dot_general(
            pick[rest, 7 * LANES :], xe[rows, LANES:], NT, preferred_element_type=f32
        )
        for i in range(n):
            state[r + i] = got[:, i * LANES : (i + 1) * LANES]

    def emit(r, value):
        fin_b[r * LANES : (r + 1) * LANES, :] = value

    run_chemistry(groups, species, LIT_CAP - FIRST, CHUNK_SECOND, mix, tab, state, made, emit)

    def settle(j, got, moved):
        keep = lit_mask[j : j + 1, :]
        back[pl.ds(j, width, stride=8), :] = jnp.where(keep, got, moved.astype(f32))

    for j in range(1, 7, 2):
        cols = slice(j * LANES, (j + 2) * LANES)
        got = jnp.dot(fin[...], pick[:FIRST, cols], preferred_element_type=f32)
        got = got + jnp.dot(fin_b[...], pick[rest, cols], preferred_element_type=f32)
        settle(j, got[:, :LANES], xb[:, j * LANES : (j + 1) * LANES])
        settle(j + 1, got[:, LANES:], xb[:, (j + 1) * LANES : (j + 2) * LANES])
    for i, j in enumerate((0, 7)):
        got = jnp.dot(
            fin_b[...], pick[rest, j * LANES : (j + 1) * LANES], preferred_element_type=f32
        )
        settle(j, got, xe[:, i * LANES : (i + 1) * LANES])

    def finish(k, base):
        for s in range(species):
            at = pl.multiple_of((base + s) * 8, 8)
            out[s * levels + k] = back[pl.ds(at, 8), :].astype(bf16)

    whole_slots = levels // groups

    def finish_body(j, carry):
        for r in range(groups):
            finish(j * groups + r, r * LANES + j * species)
        return carry

    lax.fori_loop(0, whole_slots, finish_body, 0)
    for r in range(levels - whole_slots * groups):
        finish(whole_slots * groups + r, r * LANES + whole_slots * species)


def local(tracers, east_wind, north_wind, sunlit, coupling, rate_table, rate_index, kappa):
    species, levels, lat_rows, lon_cols = tracers.shape
    slots = LANES // species
    groups = -(-levels // slots)
    width = groups * LANES
    sizes = (species, levels, groups)
    tr = tracers.reshape(species * levels, lat_rows, lon_cols)
    vmem = pl.BlockSpec(memory_space=pltpu.VMEM)
    smem = pl.BlockSpec(memory_space=pltpu.SMEM)
    shape = jax.ShapeDtypeStruct
    lon_pack, send_a, send_b, top, wind = pl.pallas_call(
        functools.partial(edge_kernel, *sizes),
        out_shape=(
            shape((species + 1, 8, LANES), bf16),
            shape((width + levels, LANES), bf16),
            shape((width + levels, LANES), bf16),
            shape((width, LANES), bf16),
            shape((levels, LANES), bf16),
        ),
        in_specs=[vmem] * 3,
        out_specs=(vmem,) * 5,
        scratch_shapes=[
            pltpu.VMEM((width * 8, LANES), f32),
            pltpu.VMEM((levels * 8, LANES), f32),
        ],
        name="edges",
    )(tr, east_wind, north_wind)

    nlon, nlat = lax.axis_size("lon"), lax.axis_size("lat")
    pairs = [(i, i ^ 1) for i in range(nlon)]
    others = [(i, (i + 1) % nlon if i % 2 else (i - 1) % nlon) for i in range(nlon)]
    lon_a = lax.ppermute(lon_pack, "lon", pairs)
    lon_b = lax.ppermute(lon_pack, "lon", others)
    pairs = [(i, i ^ 1) for i in range(nlat)]
    others = [(i, i + 1 if i % 2 else i - 1) for i in range(1, nlat - 1)]
    lat_a = lax.ppermute(send_a, "lat", pairs)
    lat_b = lax.ppermute(send_b, "lat", others) if others else jnp.zeros_like(send_b)

    small = jnp.concatenate(
        [jnp.pad(coupling, ((0, 0), (0, levels - species))), rate_table, jnp.pad(kappa, (0, 1))[None]]
    )
    part, xb, pick, fin, mix, tab = pl.pallas_call(
        functools.partial(first_kernel, *sizes),
        out_shape=(
            shape((2, width, LANES), f32),
            shape((width, 8 * LANES), bf16),
            shape((LIT_CAP, 8 * LANES), bf16),
            shape((width, FIRST), bf16),
            shape((groups, 2 * LANES, 2 * LANES), bf16),
            shape((16, LANES), f32),
        ),
        in_specs=[smem] + [vmem] * 7,
        out_specs=(vmem,) * 6,
        scratch_shapes=[
            pltpu.VMEM((species + 1, 8, LANES), f32),
            pltpu.VMEM((width * 8, LANES), f32),
            pltpu.VMEM((groups, FIRST, LANES), f32),
            pltpu.VMEM((groups, FIRST, LANES), f32),
            pltpu.VMEM((species, levels), f32),
        ],
        cost_estimate=pl.CostEstimate(
            flops=20_000_000_000, bytes_accessed=8_000_000, transcendentals=0
        ),
        compiler_params=pltpu.CompilerParams(vmem_limit_bytes=VMEM_LIMIT),
        name="first",
    )(
        rate_index,
        tr,
        east_wind,
        north_wind,
        sunlit,
        lon_a,
        lon_b,
        small,
    )

    count = LIT_CAP - FIRST
    out = pl.pallas_call(
        functools.partial(second_kernel, *sizes),
        out_shape=shape((species * levels, lat_rows, lon_cols), bf16),
        in_specs=[vmem] * 11,
        out_specs=vmem,
        scratch_shapes=[
            pltpu.VMEM((width, 2 * LANES), bf16),
            pltpu.VMEM((width, count), bf16),
            pltpu.VMEM((groups, count, LANES), f32),
            pltpu.VMEM((groups, count, LANES), f32),
            pltpu.VMEM((width * 8, LANES), f32),
        ],
        compiler_params=pltpu.CompilerParams(vmem_limit_bytes=VMEM_LIMIT),
        name="second",
    )(part, top, wind, lat_a, lat_b, xb, pick, fin, mix, tab, sunlit)
    return out.reshape(tracers.shape)


def solution(mesh):
    placed = (
        P(None, None, "lat", "lon"),
        P(None, "lat", "lon"),
        P(None, "lat", "lon"),
        P("lat", "lon"),
        P(),
        P(),
        P(),
        P(),
    )
    return jax.shard_map(
        local, mesh=mesh, in_specs=placed, out_specs=P(None, None, "lat", "lon"), check_vma=False
    )
```

```python
import functools

import jax
import jax.numpy as jnp
from jax import lax
from jax.experimental import pallas as pl
from jax.experimental.pallas import tpu as pltpu
from jax.sharding import PartitionSpec as P

SUBSTEPS = 16
LANES = 128
LIT_CAP = 768
FIRST = 512
CHUNK_FIRST = 256
CHUNK_SECOND = 128
UNROLL = 5
BLOCKS = (1, 2, 3, 4, 5, 6, 0, 7)
VMEM_LIMIT = 24 << 20
NT = (((1,), (1,)), ((), ()))
f32, bf16 = jnp.float32, jnp.bfloat16


def iota(shape, axis):
    return lax.broadcasted_iota(jnp.int32, shape, axis)


def place(k, s, species, groups):
    return (k % groups) * LANES + (k // groups) * species + s


def edge_kernel(
    species,
    levels,
    groups,
    tr,
    east,
    north,
    lon_out,
    lat_a,
    lat_b,
    top_out,
    wind_out,
    rows,
    vrow,
):
    lane = iota((8, LANES), 1)
    zero = jnp.zeros((8, LANES), f32)
    for r in range(groups):
        for p in range(LANES):
            if p >= (LANES // species) * species or (p // species) * groups + r >= levels:
                rows[pl.ds((r * LANES + p) * 8, 8), :] = zero
    for k in range(levels):
        vrow[pl.ds(k * 8, 8), :] = north[k].astype(f32)
    for s in range(species + 1):
        packed = zero
        for k in range(levels):
            if s < species:
                cell = tr[s * levels + k].astype(f32)
                rows[pl.ds(place(k, s, species, groups) * 8, 8), :] = cell
            else:
                cell = east[k].astype(f32)
            here = (lane == 2 * k) | (lane == (2 * k - 1) % LANES)
            moved = pltpu.roll(cell, 2 * k, 1) if k else cell
            packed = jnp.where(here, moved, packed)
        lon_out[s] = packed.astype(bf16)
    width = groups * LANES
    is_odd = lax.axis_index("lat") % 2 > 0
    bottom = rows[pl.ds(0, width, stride=8), :]
    top = rows[pl.ds(7, width, stride=8), :]
    wind = vrow[pl.ds(0, levels, stride=8), :].astype(bf16)
    lat_a[:width] = jnp.where(is_odd, bottom, top).astype(bf16)
    lat_b[:width] = jnp.where(is_odd, top, bottom).astype(bf16)
    lat_a[width:] = wind
    lat_b[width:] = wind
    wind_out[...] = wind
    top_out[...] = top.astype(bf16)


def run_chemistry(groups, species, count, size, mix, tab, state, made, emit, beside=None):
    kappa = tab.at[8:16]

    def produce(parts, i):
        for r, q in enumerate(parts):
            high = q.astype(bf16)
            low = (q - high.astype(f32)).astype(bf16)
            pair = jnp.concatenate([high, low], axis=1)
            res = jnp.dot(pair, mix[r], preferred_element_type=f32)
            made[r, i * size : (i + 1) * size, :] = res[:, :LANES] + res[:, LANES:]

    def react(i):
        at = slice(i * size, (i + 1) * size)
        y = []
        for r in range(groups):
            q = state[r, at, :]
            y.append(made[r, at, :] / (tab[r : r + 1, :] + q * q))
        flux = []
        for r in range(groups):
            if r + 1 < groups:
                above = y[r + 1]
            else:
                above = pltpu.roll(y[0], LANES - species, 1)
            flux.append(kappa[r : r + 1, :] * (above - y[r]))
        res = []
        for r in range(groups):
            below = flux[r - 1] if r else pltpu.roll(flux[groups - 1], species, 1)
            q = y[r] + flux[r] - below
            state[r, at, :] = q
            res.append(q)
        return res

    chunks = count // size
    for i in range(chunks):
        produce([state[r, i * size : (i + 1) * size, :] for r in range(groups)], i)

    def substep(step, carry):
        if beside is not None:
            beside(step)
        for _ in range(UNROLL):
            for i in range(chunks):
                produce(react(i), i)
        return carry

    lax.fori_loop(0, (SUBSTEPS - 1) // UNROLL, substep, 0)
    for i in range(chunks):
        react(i)
    for r in range(groups):
        emit(r, state[r, :count, :].T.astype(bf16))


def tables(species, levels, groups, coupling, rate_table, kappa, rate_index, mix, tab, loss_rows):
    slots = LANES // species
    for s in range(species):
        loss_rows[s : s + 1, :] = rate_table[pl.ds(rate_index[s], 1), :]
    p = iota((LANES, species), 0)
    slot = (p * 171) >> 11
    spread = jnp.logical_and(p - slot * species == iota((LANES, species), 1), slot < slots)
    spread = spread.astype(f32)
    full = coupling[...] + (iota((species, species), 0) == iota((species, species), 1)).astype(f32)
    same = ((iota((LANES, LANES), 0) * 171) >> 11) == ((iota((LANES, LANES), 1) * 171) >> 11)

    def block(part):
        half = lax.dot_general(spread, part.astype(f32), NT, preferred_element_type=f32)
        wide = lax.dot_general(half, spread, NT, preferred_element_type=f32)
        return jnp.where(same, wide, 0.0)

    high = full.astype(bf16)
    whole = block(high) + block((full - high.astype(f32)).astype(bf16))
    width = groups * LANES
    col = iota((levels, width), 1)
    lane = col & (LANES - 1)
    slot = (lane * 171) >> 11
    sel = jnp.logical_and(iota((levels, width), 0) == slot * groups + (col >> 7), slot < slots)
    sel = sel.astype(f32)
    exact = lax.Precision.HIGHEST
    spread_loss = jnp.dot(loss_rows[...], sel, preferred_element_type=f32, precision=exact)
    col = iota((species, width), 1) & (LANES - 1)
    mine = col - ((col * 171) >> 11) * species == iota((species, width), 0)
    loss = jnp.sum(jnp.where(mine, spread_loss, 0.0), axis=0, keepdims=True)
    kap = jnp.dot(kappa[...], sel[: levels - 1], preferred_element_type=f32, precision=exact)
    inverse = jnp.where(loss > 0.0, 1.0 / jnp.where(loss > 0.0, loss, 1.0), 0.0)
    for r in range(groups):
        mine = inverse[:, r * LANES : (r + 1) * LANES]
        tab[r : r + 1, :] = 1.0 + mine
        tab[8 + r : 9 + r, :] = kap[:, r * LANES : (r + 1) * LANES]
        scaled = whole * mine
        high = scaled.astype(bf16)
        low = (scaled - high.astype(f32)).astype(bf16)
        for at in (0, LANES):
            mix[r, at : at + LANES, :LANES] = high
            mix[r, at : at + LANES, LANES:] = low


def first_kernel(
    species,
    levels,
    groups,
    rate_index,
    tr,
    east,
    north,
    lit,
    lon_a,
    lon_b,
    coupling,
    rate_table,
    kappa,
    part_out,
    xb,
    pick,
    fin,
    mix,
    tab,
    lon_edge,
    adv,
    state,
    made,
    loss_rows,
):
    lane = iota((8, LANES), 1)
    sub = iota((8, LANES), 0)
    width = groups * LANES
    slots = LANES // species

    tables(
        species, levels, groups, coupling, rate_table, kappa, rate_index, mix, tab, loss_rows
    )
    is_odd = lax.axis_index("lon") % 2 > 0
    for s in range(species + 1):
        got_a, got_b = lon_a[s].astype(f32), lon_b[s].astype(f32)
        from_east = jnp.where(is_odd, got_b, got_a)
        from_west = jnp.where(is_odd, got_a, got_b)
        lon_edge[s] = jnp.where(lane % 2 == 0, from_east, pltpu.roll(from_west, 2, 1))
    at_pole = lax.axis_index("lat") == 0

    zero_tile = jnp.zeros((8, LANES), f32)
    for r in range(groups):
        for p in range(LANES):
            if p >= slots * species or (p // species) * groups + r >= levels:
                adv[pl.ds((r * LANES + p) * 8, 8), :] = zero_tile

    def level(k, base):
        turn = LANES - 1 - 2 * k
        u = east[k].astype(f32)
        v = north[k].astype(f32)
        v = jnp.where(jnp.logical_and(at_pole, sub == 0), 0.0, v)
        u_next = jnp.where(
            lane == LANES - 1, pltpu.roll(lon_edge[species], turn, 1), pltpu.roll(u, LANES - 1, 1)
        )
        v_next = jnp.where(sub == 7, 0.0, pltpu.roll(v, 7, 0))
        a_west = jnp.maximum(u, 0.0)
        a_east = -jnp.minimum(u_next, 0.0)
        a_south = jnp.where(sub == 0, 0.0, jnp.maximum(v, 0.0))
        a_north = -jnp.minimum(v_next, 0.0)
        a_here = (
            1.0
            - (jnp.maximum(u_next, 0.0) - jnp.minimum(u, 0.0))
            - (jnp.maximum(v_next, 0.0) - jnp.minimum(v, 0.0))
        )
        for s in range(species):
            c = tr[s * levels + k].astype(f32)
            edge = pltpu.roll(lon_edge[s], turn, 1)
            west = jnp.where(lane == 0, edge, pltpu.roll(c, 1, 1))
            east_c = jnp.where(lane == LANES - 1, edge, pltpu.roll(c, LANES - 1, 1))
            new = (
                a_here * c
                + a_west * west
                + a_east * east_c
                + a_south * pltpu.roll(c, 1, 0)
                + a_north * pltpu.roll(c, 7, 0)
            )
            at = pl.multiple_of((base + s) * 8, 8)
            adv[pl.ds(at, 8), :] = new

    whole_slots = levels // groups

    def slot_body(j, carry):
        for r in range(groups):
            level(j * groups + r, r * LANES + j * species)
        return carry

    lax.fori_loop(0, whole_slots, slot_body, 0)
    for r in range(levels - whole_slots * groups):
        level(whole_slots * groups + r, r * LANES + whole_slots * species)

    lit_mask = lit[...] > 0
    inner = jnp.logical_and(sub > 0, sub < 7)
    upper = (iota((LANES, LANES), 0) <= iota((LANES, LANES), 1)).astype(f32)
    lower = (iota((8, 8), 0) > iota((8, 8), 1)).astype(f32)

    def rank_of(mask):
        ones = mask.astype(f32)
        within = jnp.dot(ones, upper, preferred_element_type=f32)
        before = jnp.sum(jnp.dot(lower, ones, preferred_element_type=f32), axis=1, keepdims=True)
        return within + before - 1.0

    inner_rank = rank_of(jnp.logical_and(lit_mask, inner))
    outer_lit = jnp.logical_and(lit_mask, jnp.logical_not(inner))
    outer_rank = rank_of(outer_lit)
    outer_count = jnp.sum(outer_lit.astype(f32))
    slot = jnp.where(
        inner,
        inner_rank + jnp.where(inner_rank >= FIRST, outer_count, 0.0),
        outer_rank + FIRST,
    )
    slot = jnp.where(lit_mask, slot, -1.0).astype(jnp.int32)

    order = iota((LIT_CAP, LANES), 0)
    for i, j in enumerate(BLOCKS):
        pick[:, i * LANES : (i + 1) * LANES] = (
            (order == slot[j : j + 1, :]).astype(f32).astype(bf16)
        )
        rows = adv[pl.ds(j, width, stride=8), :]
        if i < 6:
            xb[:, i * LANES : (i + 1) * LANES] = rows.astype(bf16)
        else:
            part_out[i - 6] = rows

    span = slice(0, 6 * LANES)
    for r in range(0, groups, 2):
        n = min(2, groups - r)
        got = lax.dot_general(
            pick[:FIRST, span],
            xb[r * LANES : (r + n) * LANES, :],
            NT,
            preferred_element_type=f32,
        )
        for i in range(n):
            state[r + i] = got[:, i * LANES : (i + 1) * LANES]

    def emit(r, value):
        fin[r * LANES : (r + 1) * LANES, :] = value

    run_chemistry(groups, species, FIRST, CHUNK_FIRST, mix, tab, state, made, emit)


def second_kernel(
    species,
    levels,
    groups,
    part,
    top,
    wind,
    lat_a,
    lat_b,
    xb,
    pick,
    fin,
    mix,
    tab,
    lit,
    out,
    xe,
    fin_b,
    state,
    made,
    back,
    done,
    sent,
):
    width = groups * LANES
    slots = LANES // species
    lit_mask = lit[...] > 0
    row = iota((width, levels), 0)
    slot = ((row & (LANES - 1)) * 171) >> 11
    sel = jnp.logical_and(iota((width, levels), 1) == slot * groups + (row >> 7), slot < slots)
    sel = sel.astype(f32).astype(bf16)
    is_odd = lax.axis_index("lat") % 2 > 0
    got_a, got_b = lat_a[:width].astype(f32), lat_b[:width].astype(f32)
    south = jnp.where(is_odd, got_a, got_b)
    north = jnp.where(is_odd, got_b, got_a)
    v_here = jnp.dot(sel, wind[...], preferred_element_type=f32)
    v_here = jnp.where(lax.axis_index("lat") == 0, 0.0, jnp.maximum(v_here, 0.0))
    xe[:, :LANES] = (part[0] + v_here * south).astype(bf16)
    wind_a, wind_b = lat_a[width:].astype(f32), lat_b[width:].astype(f32)
    v_next = jnp.where(is_odd, wind_b, wind_a).astype(bf16)
    v_next = jnp.dot(sel, v_next, preferred_element_type=f32)
    xe[:, LANES:] = (
        part[1] - jnp.maximum(v_next, 0.0) * top[...].astype(f32) - jnp.minimum(v_next, 0.0) * north
    ).astype(bf16)

    rest = slice(FIRST, LIT_CAP)
    for r in range(0, groups, 2):
        n = min(2, groups - r)
        rows = slice(r * LANES, (r + n) * LANES)
        got = lax.dot_general(
            pick[rest, : 6 * LANES], xb[rows, :], NT, preferred_element_type=f32
        )
        got = got + lax.dot_general(
            pick[rest, 6 * LANES :], xe[rows, :], NT, preferred_element_type=f32
        )
        for i in range(n):
            state[r + i] = got[:, i * LANES : (i + 1) * LANES]

    def emit(r, value):
        fin_b[r * LANES : (r + 1) * LANES, :] = value

    def scatter_first(step):
        at = pl.multiple_of(step * 2 * LANES, 2 * LANES)
        got = jnp.dot(fin[...], pick[:FIRST, pl.ds(at, 2 * LANES)], preferred_element_type=f32)
        for i in range(2):
            back[pl.ds(2 * step + 1 + i, width, stride=8), :] = got[:, i * LANES : (i + 1) * LANES]

    run_chemistry(
        groups,
        species,
        LIT_CAP - FIRST,
        CHUNK_SECOND,
        mix,
        tab,
        state,
        made,
        emit,
        scatter_first,
    )

    def settle(j, got, moved):
        keep = lit_mask[j : j + 1, :]
        back[pl.ds(j, width, stride=8), :] = jnp.where(keep, got, moved.astype(f32))

    for i in range(0, 8, 2):
        cols = slice(i * LANES, (i + 2) * LANES)
        got = jnp.dot(fin_b[...], pick[rest, cols], preferred_element_type=f32)
        for h in range(2):
            half = got[:, h * LANES : (h + 1) * LANES]
            j = BLOCKS[i + h]
            if i < 6:
                half = half + back[pl.ds(j, width, stride=8), :]
                settle(j, half, xb[:, (i + h) * LANES : (i + h + 1) * LANES])
            else:
                settle(j, half, xe[:, h * LANES : (h + 1) * LANES])

    whole_slots = levels // groups
    parts = 4
    each = species // parts
    copies = []
    for part_at in range(parts):

        def finish(k, base):
            for s in range(part_at * each, (part_at + 1) * each):
                at = pl.multiple_of((base + s) * 8, 8)
                done[s * levels + k] = back[pl.ds(at, 8), :].astype(bf16)

        def finish_body(j, carry):
            for r in range(groups):
                finish(j * groups + r, r * LANES + j * species)
            return carry

        lax.fori_loop(0, whole_slots, finish_body, 0)
        for r in range(levels - whole_slots * groups):
            finish(whole_slots * groups + r, r * LANES + whole_slots * species)
        span = pl.ds(part_at * each * levels, each * levels)
        copies.append(pltpu.make_async_copy(done.at[span], out.at[span], sent.at[part_at]))
        copies[-1].start()
    for copy in copies:
        copy.wait()


def local(tracers, east_wind, north_wind, sunlit, coupling, rate_table, rate_index, kappa):
    species, levels, lat_rows, lon_cols = tracers.shape
    slots = LANES // species
    groups = -(-levels // slots)
    width = groups * LANES
    sizes = (species, levels, groups)
    tr = tracers.reshape(species * levels, lat_rows, lon_cols)
    vmem = pl.BlockSpec(memory_space=pltpu.VMEM)
    smem = pl.BlockSpec(memory_space=pltpu.SMEM)
    shape = jax.ShapeDtypeStruct
    lon_pack, send_a, send_b, top, wind = pl.pallas_call(
        functools.partial(edge_kernel, *sizes),
        out_shape=(
            shape((species + 1, 8, LANES), bf16),
            shape((width + levels, LANES), bf16),
            shape((width + levels, LANES), bf16),
            shape((width, LANES), bf16),
            shape((levels, LANES), bf16),
        ),
        in_specs=[vmem] * 3,
        out_specs=(vmem,) * 5,
        scratch_shapes=[
            pltpu.VMEM((width * 8, LANES), f32),
            pltpu.VMEM((levels * 8, LANES), f32),
        ],
        name="edges",
    )(tr, east_wind, north_wind)

    nlon, nlat = lax.axis_size("lon"), lax.axis_size("lat")
    pairs = [(i, i ^ 1) for i in range(nlon)]
    others = [(i, (i + 1) % nlon if i % 2 else (i - 1) % nlon) for i in range(nlon)]
    lon_a = lax.ppermute(lon_pack, "lon", pairs)
    lon_b = lax.ppermute(lon_pack, "lon", others)
    pairs = [(i, i ^ 1) for i in range(nlat)]
    others = [(i, i + 1 if i % 2 else i - 1) for i in range(1, nlat - 1)]
    lat_a = lax.ppermute(send_a, "lat", pairs)
    lat_b = lax.ppermute(send_b, "lat", others) if others else jnp.zeros_like(send_b)

    part, xb, pick, fin, mix, tab = pl.pallas_call(
        functools.partial(first_kernel, *sizes),
        out_shape=(
            shape((2, width, LANES), f32),
            shape((width, 6 * LANES), bf16),
            shape((LIT_CAP, 8 * LANES), bf16),
            shape((width, FIRST), bf16),
            shape((groups, 2 * LANES, 2 * LANES), bf16),
            shape((16, LANES), f32),
        ),
        in_specs=[smem] + [vmem] * 9,
        out_specs=(vmem,) * 6,
        scratch_shapes=[
            pltpu.VMEM((species + 1, 8, LANES), f32),
            pltpu.VMEM((width * 8, LANES), f32),
            pltpu.VMEM((groups, FIRST, LANES), f32),
            pltpu.VMEM((groups, FIRST, LANES), f32),
            pltpu.VMEM((species, levels), f32),
        ],
        cost_estimate=pl.CostEstimate(
            flops=20_000_000_000, bytes_accessed=8_000_000, transcendentals=0
        ),
        compiler_params=pltpu.CompilerParams(vmem_limit_bytes=VMEM_LIMIT),
        name="first",
    )(
        rate_index,
        tr,
        east_wind,
        north_wind,
        sunlit,
        lon_a,
        lon_b,
        coupling,
        rate_table,
        kappa.reshape(1, levels - 1),
    )

    count = LIT_CAP - FIRST
    out = pl.pallas_call(
        functools.partial(second_kernel, *sizes),
        out_shape=shape((species * levels, lat_rows, lon_cols), bf16),
        in_specs=[vmem] * 11,
        out_specs=pl.BlockSpec(memory_space=pltpu.HBM),
        scratch_shapes=[
            pltpu.VMEM((width, 2 * LANES), bf16),
            pltpu.VMEM((width, count), bf16),
            pltpu.VMEM((groups, count, LANES), f32),
            pltpu.VMEM((groups, count, LANES), f32),
            pltpu.VMEM((width * 8, LANES), f32),
            pltpu.VMEM((species * levels, lat_rows, LANES), bf16),
            pltpu.SemaphoreType.DMA((4,)),
        ],
        compiler_params=pltpu.CompilerParams(vmem_limit_bytes=VMEM_LIMIT),
        name="second",
    )(part, top, wind, lat_a, lat_b, xb, pick, fin, mix, tab, sunlit)
    return out.reshape(tracers.shape)


def solution(mesh):
    placed = (
        P(None, None, "lat", "lon"),
        P(None, "lat", "lon"),
        P(None, "lat", "lon"),
        P("lat", "lon"),
        P(),
        P(),
        P(),
        P(),
    )
    return jax.shard_map(
        local, mesh=mesh, in_specs=placed, out_specs=P(None, None, "lat", "lon"), check_vma=False
    )
```

```python
import functools

import jax
import jax.numpy as jnp
from jax import lax
from jax.experimental import pallas as pl
from jax.experimental.pallas import tpu as pltpu
from jax.sharding import PartitionSpec as P

SUBSTEPS = 16
LANES = 128
LIT_CAP = 768
FIRST = 512
CHUNK_FIRST = 256
CHUNK_SECOND = 128
UNROLL = 5
BLOCKS = (1, 2, 3, 4, 5, 6, 0, 7)
VMEM_LIMIT = 24 << 20
NT = (((1,), (1,)), ((), ()))
f32, bf16 = jnp.float32, jnp.bfloat16


def iota(shape, axis):
    return lax.broadcasted_iota(jnp.int32, shape, axis)


def place(k, s, species, groups):
    return (k % groups) * LANES + (k // groups) * species + s


def edge_kernel(
    species,
    levels,
    groups,
    tr,
    east,
    north,
    lon_out,
    lat_a,
    lat_b,
    top_out,
    wind_out,
    rows,
    vrow,
):
    lane = iota((8, LANES), 1)
    zero = jnp.zeros((8, LANES), f32)
    for r in range(groups):
        for p in range(LANES):
            if p >= (LANES // species) * species or (p // species) * groups + r >= levels:
                rows[pl.ds((r * LANES + p) * 8, 8), :] = zero
    for k in range(levels):
        vrow[pl.ds(k * 8, 8), :] = north[k].astype(f32)
    for s in range(species + 1):
        packed = zero
        for k in range(levels):
            if s < species:
                cell = tr[s * levels + k].astype(f32)
                rows[pl.ds(place(k, s, species, groups) * 8, 8), :] = cell
            else:
                cell = east[k].astype(f32)
            here = (lane == 2 * k) | (lane == (2 * k - 1) % LANES)
            moved = pltpu.roll(cell, 2 * k, 1) if k else cell
            packed = jnp.where(here, moved, packed)
        lon_out[s] = packed.astype(bf16)
    width = groups * LANES
    is_odd = lax.axis_index("lat") % 2 > 0
    bottom = rows[pl.ds(0, width, stride=8), :]
    top = rows[pl.ds(7, width, stride=8), :]
    wind = vrow[pl.ds(0, levels, stride=8), :].astype(bf16)
    lat_a[:width] = jnp.where(is_odd, bottom, top).astype(bf16)
    lat_b[:width] = jnp.where(is_odd, top, bottom).astype(bf16)
    lat_a[width:] = wind
    lat_b[width:] = wind
    wind_out[...] = wind
    top_out[...] = top.astype(bf16)


def run_chemistry(groups, species, count, size, mix, tab, state, made, emit, beside=None):
    kappa = tab.at[8:16]

    def produce(parts, i):
        for r, q in enumerate(parts):
            high = q.astype(bf16)
            low = (q - high.astype(f32)).astype(bf16)
            pair = jnp.concatenate([high, low], axis=1)
            res = jnp.dot(pair, mix[r], preferred_element_type=f32)
            made[r, i * size : (i + 1) * size, :] = res[:, :LANES] + res[:, LANES:]

    def react(i):
        at = slice(i * size, (i + 1) * size)
        y = []
        for r in range(groups):
            q = state[r, at, :]
            y.append(made[r, at, :] / (tab[r : r + 1, :] + q * q))
        flux = []
        for r in range(groups):
            if r + 1 < groups:
                above = y[r + 1]
            else:
                above = pltpu.roll(y[0], LANES - species, 1)
            flux.append(kappa[r : r + 1, :] * (above - y[r]))
        res = []
        for r in range(groups):
            below = flux[r - 1] if r else pltpu.roll(flux[groups - 1], species, 1)
            q = y[r] + flux[r] - below
            state[r, at, :] = q
            res.append(q)
        return res

    chunks = count // size
    for i in range(chunks):
        produce([state[r, i * size : (i + 1) * size, :] for r in range(groups)], i)

    def substep(step, carry):
        if beside is not None:
            beside(step)
        for _ in range(UNROLL):
            for i in range(chunks):
                produce(react(i), i)
        return carry

    lax.fori_loop(0, (SUBSTEPS - 1) // UNROLL, substep, 0)
    for i in range(chunks):
        react(i)
    for r in range(groups):
        emit(r, state[r, :count, :].T.astype(bf16))


def tables(species, levels, groups, coupling, rate_table, kappa, rate_index, mix, tab, loss_rows):
    slots = LANES // species
    for s in range(species):
        loss_rows[s : s + 1, :] = rate_table[pl.ds(rate_index[s], 1), :]
    p = iota((LANES, species), 0)
    slot = (p * 171) >> 11
    spread = jnp.logical_and(p - slot * species == iota((LANES, species), 1), slot < slots)
    spread = spread.astype(f32)
    full = coupling[...] + (iota((species, species), 0) == iota((species, species), 1)).astype(f32)
    same = ((iota((LANES, LANES), 0) * 171) >> 11) == ((iota((LANES, LANES), 1) * 171) >> 11)

    def block(part):
        half = lax.dot_general(spread, part.astype(f32), NT, preferred_element_type=f32)
        wide = lax.dot_general(half, spread, NT, preferred_element_type=f32)
        return jnp.where(same, wide, 0.0)

    high = full.astype(bf16)
    whole = block(high) + block((full - high.astype(f32)).astype(bf16))
    width = groups * LANES
    col = iota((levels, width), 1)
    lane = col & (LANES - 1)
    slot = (lane * 171) >> 11
    sel = jnp.logical_and(iota((levels, width), 0) == slot * groups + (col >> 7), slot < slots)
    sel = sel.astype(f32)
    exact = lax.Precision.HIGHEST
    spread_loss = jnp.dot(loss_rows[...], sel, preferred_element_type=f32, precision=exact)
    col = iota((species, width), 1) & (LANES - 1)
    mine = col - ((col * 171) >> 11) * species == iota((species, width), 0)
    loss = jnp.sum(jnp.where(mine, spread_loss, 0.0), axis=0, keepdims=True)
    kap = jnp.dot(kappa[...], sel[: levels - 1], preferred_element_type=f32, precision=exact)
    inverse = jnp.where(loss > 0.0, 1.0 / jnp.where(loss > 0.0, loss, 1.0), 0.0)
    for r in range(groups):
        mine = inverse[:, r * LANES : (r + 1) * LANES]
        tab[r : r + 1, :] = 1.0 + mine
        tab[8 + r : 9 + r, :] = kap[:, r * LANES : (r + 1) * LANES]
        scaled = whole * mine
        high = scaled.astype(bf16)
        low = (scaled - high.astype(f32)).astype(bf16)
        for at in (0, LANES):
            mix[r, at : at + LANES, :LANES] = high
            mix[r, at : at + LANES, LANES:] = low


def first_kernel(
    species,
    levels,
    groups,
    rate_index,
    tr,
    east,
    north,
    lit,
    lon_a,
    lon_b,
    coupling,
    rate_table,
    kappa,
    part_out,
    xb,
    pick,
    fin,
    mix,
    tab,
    lon_edge,
    adv,
    state,
    made,
    loss_rows,
):
    lane = iota((8, LANES), 1)
    sub = iota((8, LANES), 0)
    width = groups * LANES
    slots = LANES // species

    tables(
        species, levels, groups, coupling, rate_table, kappa, rate_index, mix, tab, loss_rows
    )
    is_odd = lax.axis_index("lon") % 2 > 0
    for s in range(species + 1):
        got_a, got_b = lon_a[s].astype(f32), lon_b[s].astype(f32)
        from_east = jnp.where(is_odd, got_b, got_a)
        from_west = jnp.where(is_odd, got_a, got_b)
        lon_edge[s] = jnp.where(lane % 2 == 0, from_east, pltpu.roll(from_west, 2, 1))
    at_pole = lax.axis_index("lat") == 0

    zero_tile = jnp.zeros((8, LANES), f32)
    for r in range(groups):
        for p in range(LANES):
            if p >= slots * species or (p // species) * groups + r >= levels:
                adv[pl.ds((r * LANES + p) * 8, 8), :] = zero_tile

    def level(k, base):
        turn = LANES - 1 - 2 * k
        u = east[k].astype(f32)
        v = north[k].astype(f32)
        v = jnp.where(jnp.logical_and(at_pole, sub == 0), 0.0, v)
        u_next = jnp.where(
            lane == LANES - 1, pltpu.roll(lon_edge[species], turn, 1), pltpu.roll(u, LANES - 1, 1)
        )
        v_next = jnp.where(sub == 7, 0.0, pltpu.roll(v, 7, 0))
        a_west = jnp.maximum(u, 0.0)
        a_east = jnp.minimum(u_next, 0.0)
        a_south = jnp.where(sub == 0, 0.0, jnp.maximum(v, 0.0))
        a_north = jnp.minimum(v_next, 0.0)
        a_here = (
            1.0
            - (jnp.maximum(u_next, 0.0) - jnp.minimum(u, 0.0))
            - (jnp.maximum(v_next, 0.0) - jnp.minimum(v, 0.0))
        )
        for s in range(species):
            c = tr[s * levels + k].astype(f32)
            edge = pltpu.roll(lon_edge[s], turn, 1)
            west = jnp.where(lane == 0, edge, pltpu.roll(c, 1, 1))
            east_c = jnp.where(lane == LANES - 1, edge, pltpu.roll(c, LANES - 1, 1))
            new = (
                a_here * c
                + a_west * west
                - a_east * east_c
                + a_south * pltpu.roll(c, 1, 0)
                - a_north * pltpu.roll(c, 7, 0)
            )
            at = pl.multiple_of((base + s) * 8, 8)
            adv[pl.ds(at, 8), :] = new

    whole_slots = levels // groups

    def slot_body(j, carry):
        for r in range(groups):
            level(j * groups + r, r * LANES + j * species)
        return carry

    lax.fori_loop(0, whole_slots, slot_body, 0)
    for r in range(levels - whole_slots * groups):
        level(whole_slots * groups + r, r * LANES + whole_slots * species)

    lit_mask = lit[...] > 0
    inner = jnp.logical_and(sub > 0, sub < 7)
    upper = (iota((LANES, LANES), 0) <= iota((LANES, LANES), 1)).astype(f32)
    lower = (iota((8, 8), 0) > iota((8, 8), 1)).astype(f32)

    def rank_of(mask):
        ones = mask.astype(f32)
        within = jnp.dot(ones, upper, preferred_element_type=f32)
        before = jnp.sum(jnp.dot(lower, ones, preferred_element_type=f32), axis=1, keepdims=True)
        return within + before - 1.0

    inner_rank = rank_of(jnp.logical_and(lit_mask, inner))
    outer_lit = jnp.logical_and(lit_mask, jnp.logical_not(inner))
    outer_rank = rank_of(outer_lit)
    outer_count = jnp.sum(outer_lit.astype(f32))
    slot = jnp.where(
        inner,
        inner_rank + jnp.where(inner_rank >= FIRST, outer_count, 0.0),
        outer_rank + FIRST,
    )
    slot = jnp.where(lit_mask, slot, -1.0).astype(jnp.int32)

    order = iota((LIT_CAP, LANES), 0)
    for i, j in enumerate(BLOCKS):
        pick[:, i * LANES : (i + 1) * LANES] = (
            (order == slot[j : j + 1, :]).astype(f32).astype(bf16)
        )
        rows = adv[pl.ds(j, width, stride=8), :]
        if i < 6:
            xb[:, i * LANES : (i + 1) * LANES] = rows.astype(bf16)
        else:
            part_out[i - 6] = rows

    span = slice(0, 6 * LANES)
    for r in range(0, groups, 2):
        n = min(2, groups - r)
        got = lax.dot_general(
            pick[:FIRST, span],
            xb[r * LANES : (r + n) * LANES, :],
            NT,
            preferred_element_type=f32,
        )
        for i in range(n):
            state[r + i] = got[:, i * LANES : (i + 1) * LANES]

    def emit(r, value):
        fin[r * LANES : (r + 1) * LANES, :] = value

    run_chemistry(groups, species, FIRST, CHUNK_FIRST, mix, tab, state, made, emit)


def second_kernel(
    species,
    levels,
    groups,
    part,
    top,
    wind,
    lat_a,
    lat_b,
    xb,
    pick,
    fin,
    mix,
    tab,
    lit,
    out,
    xe,
    fin_b,
    state,
    made,
    back,
    done,
    sent,
):
    width = groups * LANES
    slots = LANES // species
    lit_mask = lit[...] > 0
    row = iota((width, levels), 0)
    slot = ((row & (LANES - 1)) * 171) >> 11
    sel = jnp.logical_and(iota((width, levels), 1) == slot * groups + (row >> 7), slot < slots)
    sel = sel.astype(f32).astype(bf16)
    is_odd = lax.axis_index("lat") % 2 > 0
    got_a, got_b = lat_a[:width].astype(f32), lat_b[:width].astype(f32)
    south = jnp.where(is_odd, got_a, got_b)
    north = jnp.where(is_odd, got_b, got_a)
    v_here = jnp.dot(sel, wind[...], preferred_element_type=f32)
    v_here = jnp.where(lax.axis_index("lat") == 0, 0.0, jnp.maximum(v_here, 0.0))
    xe[:, :LANES] = (part[0] + v_here * south).astype(bf16)
    wind_a, wind_b = lat_a[width:].astype(f32), lat_b[width:].astype(f32)
    v_next = jnp.where(is_odd, wind_b, wind_a).astype(bf16)
    v_next = jnp.dot(sel, v_next, preferred_element_type=f32)
    xe[:, LANES:] = (
        part[1] - jnp.maximum(v_next, 0.0) * top[...].astype(f32) - jnp.minimum(v_next, 0.0) * north
    ).astype(bf16)

    rest = slice(FIRST, LIT_CAP)
    for r in range(0, groups, 2):
        n = min(2, groups - r)
        rows = slice(r * LANES, (r + n) * LANES)
        got = lax.dot_general(
            pick[rest, : 6 * LANES], xb[rows, :], NT, preferred_element_type=f32
        )
        got = got + lax.dot_general(
            pick[rest, 6 * LANES :], xe[rows, :], NT, preferred_element_type=f32
        )
        for i in range(n):
            state[r + i] = got[:, i * LANES : (i + 1) * LANES]

    def emit(r, value):
        fin_b[r * LANES : (r + 1) * LANES, :] = value

    def scatter_first(step):
        at = pl.multiple_of(step * 2 * LANES, 2 * LANES)
        got = jnp.dot(fin[...], pick[:FIRST, pl.ds(at, 2 * LANES)], preferred_element_type=f32)
        for i in range(2):
            back[pl.ds(2 * step + 1 + i, width, stride=8), :] = got[:, i * LANES : (i + 1) * LANES]

    run_chemistry(
        groups,
        species,
        LIT_CAP - FIRST,
        CHUNK_SECOND,
        mix,
        tab,
        state,
        made,
        emit,
        scatter_first,
    )

    def settle(j, got, moved):
        keep = lit_mask[j : j + 1, :]
        back[pl.ds(j, width, stride=8), :] = jnp.where(keep, got, moved.astype(f32))

    for i in range(0, 8, 2):
        cols = slice(i * LANES, (i + 2) * LANES)
        got = jnp.dot(fin_b[...], pick[rest, cols], preferred_element_type=f32)
        for h in range(2):
            half = got[:, h * LANES : (h + 1) * LANES]
            j = BLOCKS[i + h]
            if i < 6:
                half = half + back[pl.ds(j, width, stride=8), :]
                settle(j, half, xb[:, (i + h) * LANES : (i + h + 1) * LANES])
            else:
                settle(j, half, xe[:, h * LANES : (h + 1) * LANES])

    whole_slots = levels // groups
    parts = 4
    each = species // parts
    copies = []
    for part_at in range(parts):

        def finish(k, base):
            for s in range(part_at * each, (part_at + 1) * each):
                at = pl.multiple_of((base + s) * 8, 8)
                done[s * levels + k] = back[pl.ds(at, 8), :].astype(bf16)

        def finish_body(j, carry):
            for r in range(groups):
                finish(j * groups + r, r * LANES + j * species)
            return carry

        lax.fori_loop(0, whole_slots, finish_body, 0)
        for r in range(levels - whole_slots * groups):
            finish(whole_slots * groups + r, r * LANES + whole_slots * species)
        span = pl.ds(part_at * each * levels, each * levels)
        copies.append(pltpu.make_async_copy(done.at[span], out.at[span], sent.at[part_at]))
        copies[-1].start()
    for copy in copies:
        copy.wait()


def local(tracers, east_wind, north_wind, sunlit, coupling, rate_table, rate_index, kappa):
    species, levels, lat_rows, lon_cols = tracers.shape
    slots = LANES // species
    groups = -(-levels // slots)
    width = groups * LANES
    sizes = (species, levels, groups)
    tr = tracers.reshape(species * levels, lat_rows, lon_cols)
    vmem = pl.BlockSpec(memory_space=pltpu.VMEM)
    smem = pl.BlockSpec(memory_space=pltpu.SMEM)
    shape = jax.ShapeDtypeStruct
    lon_pack, send_a, send_b, top, wind = pl.pallas_call(
        functools.partial(edge_kernel, *sizes),
        out_shape=(
            shape((species + 1, 8, LANES), bf16),
            shape((width + levels, LANES), bf16),
            shape((width + levels, LANES), bf16),
            shape((width, LANES), bf16),
            shape((levels, LANES), bf16),
        ),
        in_specs=[vmem] * 3,
        out_specs=(vmem,) * 5,
        scratch_shapes=[
            pltpu.VMEM((width * 8, LANES), f32),
            pltpu.VMEM((levels * 8, LANES), f32),
        ],
        name="edges",
    )(tr, east_wind, north_wind)

    nlon, nlat = lax.axis_size("lon"), lax.axis_size("lat")
    pairs = [(i, i ^ 1) for i in range(nlon)]
    others = [(i, (i + 1) % nlon if i % 2 else (i - 1) % nlon) for i in range(nlon)]
    lon_a = lax.ppermute(lon_pack, "lon", pairs)
    lon_b = lax.ppermute(lon_pack, "lon", others)
    pairs = [(i, i ^ 1) for i in range(nlat)]
    others = [(i, i + 1 if i % 2 else i - 1) for i in range(1, nlat - 1)]
    lat_a = lax.ppermute(send_a, "lat", pairs)
    lat_b = lax.ppermute(send_b, "lat", others) if others else jnp.zeros_like(send_b)

    part, xb, pick, fin, mix, tab = pl.pallas_call(
        functools.partial(first_kernel, *sizes),
        out_shape=(
            shape((2, width, LANES), f32),
            shape((width, 6 * LANES), bf16),
            shape((LIT_CAP, 8 * LANES), bf16),
            shape((width, FIRST), bf16),
            shape((groups, 2 * LANES, 2 * LANES), bf16),
            shape((16, LANES), f32),
        ),
        in_specs=[smem] + [vmem] * 9,
        out_specs=(vmem,) * 6,
        scratch_shapes=[
            pltpu.VMEM((species + 1, 8, LANES), f32),
            pltpu.VMEM((width * 8, LANES), f32),
            pltpu.VMEM((groups, FIRST, LANES), f32),
            pltpu.VMEM((groups, FIRST, LANES), f32),
            pltpu.VMEM((species, levels), f32),
        ],
        cost_estimate=pl.CostEstimate(
            flops=20_000_000_000, bytes_accessed=8_000_000, transcendentals=0
        ),
        compiler_params=pltpu.CompilerParams(vmem_limit_bytes=VMEM_LIMIT),
        name="first",
    )(
        rate_index,
        tr,
        east_wind,
        north_wind,
        sunlit,
        lon_a,
        lon_b,
        coupling,
        rate_table,
        kappa.reshape(1, levels - 1),
    )

    count = LIT_CAP - FIRST
    out = pl.pallas_call(
        functools.partial(second_kernel, *sizes),
        out_shape=shape((species * levels, lat_rows, lon_cols), bf16),
        in_specs=[vmem] * 11,
        out_specs=pl.BlockSpec(memory_space=pltpu.HBM),
        scratch_shapes=[
            pltpu.VMEM((width, 2 * LANES), bf16),
            pltpu.VMEM((width, count), bf16),
            pltpu.VMEM((groups, count, LANES), f32),
            pltpu.VMEM((groups, count, LANES), f32),
            pltpu.VMEM((width * 8, LANES), f32),
            pltpu.VMEM((species * levels, lat_rows, LANES), bf16),
            pltpu.SemaphoreType.DMA((4,)),
        ],
        compiler_params=pltpu.CompilerParams(vmem_limit_bytes=VMEM_LIMIT),
        name="second",
    )(part, top, wind, lat_a, lat_b, xb, pick, fin, mix, tab, sunlit)
    return out.reshape(tracers.shape)


def solution(mesh):
    placed = (
        P(None, None, "lat", "lon"),
        P(None, "lat", "lon"),
        P(None, "lat", "lon"),
        P("lat", "lon"),
        P(),
        P(),
        P(),
        P(),
    )
    return jax.shard_map(
        local, mesh=mesh, in_specs=placed, out_specs=P(None, None, "lat", "lon"), check_vma=False
    )
```
